32 devices in a mesh: atoms: 8 (over z, y), chan: 4 (over x, core).
Axes of the slice: x: 2, y: 2, z: 4, core: 2. Of those that a mesh axis runs over, the one named last changes fastest.
Arguments:
- node_x: bfloat16 [49, 128, 512], P(None, 'chan', 'atoms'), may hold values from -6 to 6
- cotangent: bfloat16 [49, 128, 512], P(None, 'chan', 'atoms'), may hold values from -6 to 6
- rotation: bfloat16 [235, 4096], P(None, 'atoms'), may hold values from -2.5 to 2.5
- envelope: float32 [4096], P('atoms'), may hold values from 0.2 to 1
- source: int32 [4096], P('atoms'), may hold values from 0 to 127, as said below
- target: int32 [4096], P('atoms'), may hold values from 0 to 63
- edge_count: int32 [8], P('atoms'), may hold values from 128 to 512, as said below
- send_index: int32 [8, 8, 8], P('atoms'), may hold values from 0 to 63
- halo_count: int32 [8, 8], P(None, 'atoms'), may hold values from 0 to 8, as said below
- weight_zero: bfloat16 [7, 128, 7, 128], P(None, 'chan'), may hold values from -0.1875 to 0.1875
- weight_one: bfloat16 [2, 6, 128, 6, 128], P(None, None, 'chan'), may hold values from -0.15625 to 0.15625
- weight_two: bfloat16 [2, 5, 128, 5, 128], P(None, None, 'chan'), may hold values from -0.15625 to 0.15625
Outputs:
- grad_x: float32 [49, 128, 512], P(None, 'chan', 'atoms')
- grad_weight_zero: float32 [7, 128, 7, 128], P(None, 'chan', None, 'atoms')
- grad_weight_one: float32 [2, 6, 128, 6, 128], P(None, None, 'chan', None, 'atoms')
- grad_weight_two: float32 [2, 5, 128, 5, 128], P(None, None, 'chan', None, 'atoms')
The draws below stay inside these ranges and needn't reach their ends.
Inputs may be any that keep to these rules, and one draw needn't show every extreme that they name: `edge_count`: at least 128 slots of each partition are live, and some partition has all 512 slots live in every draw; live slots come first. `halo_count`: A partition sends nothing to itself and between 4 and 8 atoms to every other partition; partitions whose indices differ by one, cyclically, exchange exactly 8. `source`: A value of 64 or more names slot j of sender p with p other than the edge's own partition and j below halo_count[p, own partition].
All inputs are finite; a program needn't handle non-finite values.
Results may differ from the reference program's by a relative error of at most 0.005.
Values may be sent and summed in bfloat16 or wider, within the bound.
A program may use at most 128 MiB of HBM per device.

```python
import math
import jax
import jax.numpy as jnp
from jax import lax

C = 128
ATOM_DEV = 64
HALO = 8
EDGE_DEV = 512
SECTIONS = 8
ATOMS = 512
EDGES = 4096


def draw_edge_count(key, part):
    first_key, second_key = jax.random.split(key)
    counts = jax.random.randint(first_key, (SECTIONS,), EDGE_DEV // 4, EDGE_DEV + 1)
    fullest = jax.random.randint(second_key, (), 0, SECTIONS)
    return jnp.where(jnp.arange(SECTIONS) == fullest, EDGE_DEV, counts).astype(jnp.int32)


def halo_table(key):
    table_key = jax.random.fold_in(key, 7)
    drawn = jax.random.randint(table_key, (SECTIONS, SECTIONS), HALO // 2, HALO + 1)
    rows = jnp.arange(SECTIONS, dtype=jnp.int32)[:, None]
    cols = jnp.arange(SECTIONS, dtype=jnp.int32)[None, :]
    spread = jnp.abs(rows - cols)
    apart = jnp.minimum(spread, SECTIONS - spread)
    table = jnp.where(apart == 1, HALO, drawn)
    table = jnp.where(apart == 0, 0, table)
    return table.astype(jnp.int32)


def draw_halo_count(key, part):
    return halo_table(key)


def draw_source(key, part):
    table = halo_table(key)
    base_key = jax.random.fold_in(key, 11)
    flag_key, own_key, offset_key, slot_key = jax.random.split(base_key, 4)
    own_flag = jax.random.randint(flag_key, (EDGES,), 0, 5) == 0
    own = jax.random.randint(own_key, (EDGES,), 0, ATOM_DEV)
    home = jnp.arange(EDGES, dtype=jnp.int32) // EDGE_DEV
    offset = jax.random.randint(offset_key, (EDGES,), 1, SECTIONS)
    sender = (home + offset) % SECTIONS
    slot = jax.random.randint(slot_key, (EDGES,), 0, HALO) % table[sender, home]
    halo_value = ATOM_DEV + sender * HALO + slot
    value = jnp.where(own_flag, own, halo_value)
    position = jnp.arange(EDGES, dtype=jnp.int32)
    value = jnp.where(position == 0, 0, value)
    value = jnp.where(position == 1, ATOM_DEV + SECTIONS * HALO - 1, value)
    return value.astype(jnp.int32)


def with_ends(entries, key, smallest, largest):
    index_at = [jax.random.randint(jax.random.fold_in(key, axis), (), 0, length) for axis, length in enumerate(entries.shape)]
    longest = entries.shape.index(max(entries.shape))
    neighbour = index_at[:longest] + [(index_at[longest] + 1) % entries.shape[longest]] + index_at[longest + 1:]
    return entries.at[tuple(index_at)].set(smallest).at[tuple(neighbour)].set(largest)


def levels(key, shape, cuts, least, largest):
    def one(dim, blocks):
        steps = jax.random.uniform(jax.random.fold_in(jax.random.fold_in(key, 6), dim), (blocks,), jnp.float32, least / len(cuts), largest / len(cuts))
        return jnp.repeat(jnp.exp(steps), shape[dim] // blocks).reshape((-1,) + (1,) * (len(shape) - dim - 1))

    gain = one(*cuts[0])
    for cut in cuts[1:]:
        gain = gain * one(*cut)
    return gain


def centred(key, shape, scale, bound, cuts=(), kind=jnp.bfloat16):
    gain = levels(key, shape, cuts, -0.22, 0.18) if cuts else 1.0
    entries = jax.random.normal(key, shape, jnp.float32) * scale * gain
    return jnp.minimum(jnp.maximum(entries, -bound), bound).astype(kind)


def setup_inputs(seed: int = 0) -> dict:
    streams_of = jax.random.split(jax.random.key(seed), 13)
    return {
        "node_x": centred(streams_of[0], (49, C, ATOMS), 1.0, 6.0, ((1, 4), (2, 8))),
        "cotangent": centred(streams_of[1], (49, C, ATOMS), 1.0, 6.0, ((1, 4), (2, 8))),
        "rotation": centred(streams_of[2], (235, EDGES), 0.4, 2.5, ((1, 8),)),
        "envelope": jnp.clip(0.2 + 0.8 * jax.random.uniform(streams_of[3], (EDGES,), jnp.float32) ** levels(streams_of[3], (EDGES,), ((0, 8),), -0.2, 0.2), 0.2, 1.0),
        "source": draw_source(jax.random.fold_in(streams_of[12], 71), 0),
        "target": with_ends(jax.random.randint(streams_of[5], (EDGES,), 0, ATOM_DEV), jax.random.fold_in(streams_of[5], 1), 0, ATOM_DEV - 1).astype(jnp.int32),
        "edge_count": draw_edge_count(jax.random.fold_in(streams_of[12], 71), 0),
        "send_index": with_ends(jax.random.randint(streams_of[7], (SECTIONS, SECTIONS, HALO), 0, ATOM_DEV), jax.random.fold_in(streams_of[7], 1), 0, ATOM_DEV - 1).astype(jnp.int32),
        "halo_count": draw_halo_count(jax.random.fold_in(streams_of[12], 71), 0),
        "weight_zero": centred(streams_of[9], (7, C, 7, C), (7 * C) ** -0.5, 0.1875, ((1, 4),)),
        "weight_one": centred(streams_of[10], (2, 6, C, 6, C), (12 * C) ** -0.5, 0.15625, ((2, 4),)),
        "weight_two": centred(streams_of[11], (2, 5, C, 5, C), (10 * C) ** -0.5, 0.15625, ((2, 4),)),
    }


def frame_pairs():
    listing = [(degree, 0) for degree in range(7)]
    for order in (1, 2):
        listing = listing + [(degree, order) for degree in range(order, 7)]
        listing = listing + [(degree, -order) for degree in range(order, 7)]
    return listing

def rotate_in(packed, feature):
    pieces = []
    offset = 0
    for degree in range(7):
        reach = min(degree, 2)
        height = 2 * reach + 1
        breadth = 2 * degree + 1
        matrix = packed[offset:offset + height * breadth].reshape(height, breadth, packed.shape[1])
        offset = offset + height * breadth
        part_in = feature[degree * degree:degree * degree + breadth]
        pieces.append(jnp.einsum('rke,kce->rce', matrix, part_in))
    return jnp.stack([pieces[degree][min(degree, 2) + order] for degree, order in frame_pairs()])

def rotate_out(packed, framed):
    places = {pair: index for index, pair in enumerate(frame_pairs())}
    pieces = []
    offset = 0
    for degree in range(7):
        reach = min(degree, 2)
        height = 2 * reach + 1
        breadth = 2 * degree + 1
        matrix = packed[offset:offset + height * breadth].reshape(height, breadth, packed.shape[1])
        offset = offset + height * breadth
        stacked = jnp.stack([framed[places[degree, order]] for order in range(-reach, reach + 1)])
        pieces.append(jnp.einsum('rke,rce->kce', matrix, stacked))
    return jnp.concatenate(pieces, axis=0)

def contract(weight, grads):
    first, inner, second, other = weight.shape
    count = grads.shape[2]
    product = jnp.dot(weight.reshape(first * inner, second * other), grads.reshape(second * other, count), preferred_element_type=jnp.float32)
    return product.reshape(first, inner, count)

def outer_sum(rotated, grads):
    first, inner, count = rotated.shape
    second, other = (grads.shape[0], grads.shape[1])
    product = lax.dot_general(rotated.reshape(first * inner, count), grads.reshape(second * other, count), (((1,), (1,)), ((), ())), preferred_element_type=jnp.float32)
    return product.reshape(first, inner, second, other)

def frame_backward(rotated, edge_grad, weight_zero, weight_one, weight_two):
    spans = ((0, 7), (7, 13), (13, 19), (19, 24), (24, 29))
    hpart = [rotated[start:stop] for start, stop in spans]
    gpart = [edge_grad[start:stop] for start, stop in spans]
    backs = [contract(weight_zero, gpart[0])]
    grad_zero = outer_sum(hpart[0], gpart[0])
    grads = []
    for weight, plus, minus in ((weight_one, 1, 2), (weight_two, 3, 4)):
        real_part = weight[0]
        imag_part = weight[1]
        backs.append(contract(real_part, gpart[plus]) + contract(imag_part, gpart[minus]))
        backs.append(contract(real_part, gpart[minus]) - contract(imag_part, gpart[plus]))
        grad_real = outer_sum(hpart[plus], gpart[plus]) + outer_sum(hpart[minus], gpart[minus])
        grad_imag = outer_sum(hpart[plus], gpart[minus]) - outer_sum(hpart[minus], gpart[plus])
        grads.append(jnp.stack([grad_real, grad_imag]))
    return (jnp.concatenate(backs, axis=0), grad_zero, grads[0], grads[1])

def reference(node_x, cotangent, rotation, envelope, source, target, edge_count, send_index, halo_count, weight_zero, weight_one, weight_two):
    channels = node_x.shape[1]
    grad_init = jnp.zeros((49, channels, ATOMS), jnp.float32)
    zero_init = jnp.zeros(weight_zero.shape, jnp.float32)
    one_init = jnp.zeros(weight_one.shape, jnp.float32)
    two_init = jnp.zeros(weight_two.shape, jnp.float32)

    def step(carry, partition):
        grad_all, grad_zero, grad_one, grad_two = carry
        first_slot = partition * EDGE_DEV
        source_ids = lax.dynamic_slice_in_dim(source, first_slot, EDGE_DEV)
        target_ids = lax.dynamic_slice_in_dim(target, first_slot, EDGE_DEV)
        packed = lax.dynamic_slice_in_dim(rotation, first_slot, EDGE_DEV, 1).astype(jnp.float32)
        radial = lax.dynamic_slice_in_dim(envelope, first_slot, EDGE_DEV)
        halo_slot = jnp.maximum(source_ids - ATOM_DEV, 0)
        sender = (halo_slot // HALO).astype(jnp.int32)
        within = (halo_slot % HALO).astype(jnp.int32)
        remote = send_index[sender, partition, within] + sender * ATOM_DEV
        source_atom = jnp.where(source_ids < ATOM_DEV, partition * ATOM_DEV + source_ids, remote).astype(jnp.int32)
        target_atom = (partition * ATOM_DEV + target_ids).astype(jnp.int32)
        usable = (source_ids < ATOM_DEV) | (within < halo_count[sender, partition])
        live = ((jnp.arange(EDGE_DEV, dtype=jnp.int32) < edge_count[partition]) & usable).astype(jnp.float32)
        rotated = rotate_in(packed, node_x[:, :, source_atom].astype(jnp.float32)).astype(jnp.bfloat16)
        edge_grad = (rotate_in(packed, cotangent[:, :, target_atom].astype(jnp.float32)) * (radial * live)).astype(jnp.bfloat16)
        frame_back, add_zero, add_one, add_two = frame_backward(rotated, edge_grad, weight_zero, weight_one, weight_two)
        grad_all = grad_all.at[:, :, source_atom].add(rotate_out(packed, frame_back))
        return ((grad_all, grad_zero + add_zero, grad_one + add_one, grad_two + add_two), None)
    final, unused = lax.scan(step, (grad_init, zero_init, one_init, two_init), jnp.arange(SECTIONS, dtype=jnp.int32))
    factor = 1.0 / math.sqrt(EDGES)
    return (final[0], final[1] * factor, final[2] * factor, final[3] * factor)
```

```python
import functools
import math

import jax
import jax.numpy as jnp
from jax import lax
from jax.experimental import pallas as pl
from jax.experimental.pallas import tpu as pltpu
from jax.sharding import PartitionSpec as P

LANES = 128
BF = jnp.bfloat16
F32 = jnp.float32
VMEM_LIMIT = 56 * 1024 * 1024
MESH = pl.DeviceIdType.MESH


def dot(a, b, dims):
    return lax.dot_general(a, b, (dims, ((), ())), preferred_element_type=F32)


NN = ((1,), (0,))
NT = ((1,), (1,))
TN = ((0,), (0,))


def degrees():
    offset = 0
    for degree in range(7):
        reach = min(degree, 2)
        yield degree, reach, offset
        offset += (2 * reach + 1) * (2 * degree + 1)


def cols(block, base=0):
    return pl.ds(pl.multiple_of(base + block * LANES, LANES), LANES)


def rotate_in(rot, raw, block, width, put):
    e = cols(block)
    for degree, reach, offset in degrees():
        breadth = 2 * degree + 1
        acc = [None] * (2 * reach + 1)
        for k in range(breadth):
            v = raw[pl.ds((degree * degree + k) * width, width), e]
            for r in range(2 * reach + 1):
                term = rot[pl.ds(offset + r * breadth + k, 1), e] * v
                acc[r] = term if acc[r] is None else acc[r] + term
        for r in range(2 * reach + 1):
            put(degree, r - reach, acc[r])


def rotate_out(rot, framed, block, width, out):
    e = cols(block)
    spots = {}
    for i, pair in enumerate(frame_pairs()):
        spots[pair] = i
    for degree, reach, offset in degrees():
        breadth = 2 * degree + 1
        u = [
            framed[pl.ds(spots[degree, m] * width, width), e]
            for m in range(-reach, reach + 1)
        ]
        for k in range(breadth):
            acc = None
            for r in range(2 * reach + 1):
                term = rot[pl.ds(offset + r * breadth + k, 1), e] * u[r]
                acc = term if acc is None else acc + term
            out[pl.ds((degree * degree + k) * width, width), e] = acc.astype(BF)


def frame_pairs():
    listing = [(degree, 0) for degree in range(7)]
    for order in (1, 2):
        listing = listing + [(degree, order) for degree in range(order, 7)]
        listing = listing + [(degree, -order) for degree in range(order, 7)]
    return listing


def onehot(ids, rows):
    return (lax.broadcasted_iota(jnp.int32, (rows, ids.shape[1]), 0) == ids).astype(BF)


def onehot_cols(ids, columns):
    return (lax.broadcasted_iota(jnp.int32, (ids.shape[0], columns), 1) == ids).astype(BF)


def prep_kernel(sends, node, cot, send_out, cot_out):
    atoms = node.shape[1]
    send_out[...] = dot(onehot_cols(sends[...], atoms), node[...], NT).astype(BF)
    eye = onehot_cols(lax.broadcasted_iota(jnp.int32, (atoms, 1), 0), atoms)
    cot_out[...] = dot(eye, cot[...], NT).astype(BF)


def frame_kernel(
    node,
    recv,
    cot,
    rotation,
    envelope,
    source,
    target,
    count,
    valid,
    gz,
    g1,
    g2,
    dz_out,
    d1_out,
    d2_out,
    rot,
    raw,
    radial,
    hz,
    h1,
    h2,
):
    atoms = node.shape[1]
    slots = recv.shape[0]
    edges = rotation.shape[1]
    blocks = edges // LANES
    groups = cot.shape[0]
    width = node.shape[0] // 49
    channels = gz.shape[0] // 7
    g12 = {1: g1, 2: g2}
    h12 = {1: h1, 2: h2}

    rot[...] = rotation[...].astype(F32)
    ids = source[...]
    own = onehot(ids, atoms)
    halo = onehot(ids - atoms, slots)
    usable = jnp.sum(halo.astype(F32) * valid[...], axis=0, keepdims=True)
    usable = jnp.where(ids < atoms, 1.0, usable)
    place = lax.broadcasted_iota(jnp.int32, (1, edges), 1)
    radial[...] = jnp.where(place < count[...], envelope[...] * usable, 0.0)
    to = onehot(target[...], atoms)

    def group(q, carry):
        raw[...] = dot(cot[q], to, TN)

        def one(block, carry):
            e = cols(block)
            scale = radial[:, e]

            def put(degree, m, value):
                value = (value * scale).astype(BF)
                order = abs(m)
                row = pl.ds(
                    pl.multiple_of((degree - order) * channels + q * width, width), width
                )
                if order == 0:
                    gz[row, e] = value
                else:
                    g12[order][row, cols(block, 0 if m > 0 else edges)] = value

            rotate_in(rot, raw, block, width, put)
            return carry

        return lax.fori_loop(0, blocks, one, carry)

    lax.fori_loop(0, groups, group, 0)

    raw[...] = dot(node[...], own, NN) + dot(recv[...], halo, TN)
    hz[...] = jnp.zeros_like(hz)
    h2[...] = jnp.zeros_like(h2)

    def one_h(block, carry):
        e = cols(block)
        later = cols(block, edges)

        def put(degree, m, value):
            value = value.astype(BF)
            order = abs(m)
            first = (degree - order) * width
            second = (7 - order + degree - order) * width
            if order == 0:
                hz[pl.ds(first, width), e] = value
            elif m > 0:
                h12[order][pl.ds(first, width), e] = value
                h12[order][pl.ds(second, width), later] = value
            else:
                h12[order][pl.ds(first, width), later] = value
                h12[order][pl.ds(second, width), e] = -value

        rotate_in(rot, raw, block, width, put)
        return carry

    lax.fori_loop(0, blocks, one_h, 0)

    dz_out[...] = dot(gz[...], hz[...], NT)
    d1_out[...] = dot(g1[...], h1[...], NT)
    d2_out[...] = dot(g2[...], h2[...], NT)


def back_kernel(gz, g1, g2, wz, w1, w2, rotation, source, own_out, halo_out, rot, fb, y):
    edges = rotation.shape[1]
    blocks = edges // LANES
    atoms = own_out.shape[1]
    slots = halo_out.shape[0]
    width = wz.shape[0] // 7
    rot[...] = rotation[...].astype(F32)
    fb[pl.ds(0, 7 * width), :] = dot(wz[...], gz[...], NN)
    start = 7 * width
    for count_l, w, g in ((6, w1, g1), (5, w2, g2)):
        rows = count_l * width
        real = dot(w[pl.ds(0, rows), :], g[...], NN)
        imag = dot(w[pl.ds(rows, rows), :], g[...], NN)
        fb[pl.ds(start, rows), :] = real[:, :edges] + imag[:, edges:]
        fb[pl.ds(start + rows, rows), :] = real[:, edges:] - imag[:, :edges]
        start += 2 * rows

    def one(block, carry):
        rotate_out(rot, fb, block, width, y)
        return carry

    lax.fori_loop(0, blocks, one, 0)
    ids = source[...]
    own_out[...] = dot(y[...], onehot(ids, atoms), NT)
    halo_out[...] = dot(onehot(ids - atoms, slots), y[...], NT).astype(BF)


def join_kernel(own, back, sends, out):
    out[...] = own[...] + dot(back[...], onehot_cols(sends[...], own.shape[1]), TN)


def column(row):
    n = row.shape[1]
    diag = lax.broadcasted_iota(jnp.int32, (n, n), 0) == lax.broadcasted_iota(
        jnp.int32, (n, n), 1
    )
    spread = jnp.where(diag, jnp.broadcast_to(row.astype(F32), (n, n)), 0.0)
    return jnp.sum(spread, axis=1, keepdims=True)


def whole_kernel(
    factor,
    sends_in,
    node_in,
    cot_in,
    rotation_in,
    envelope,
    source,
    target,
    count,
    counts_in,
    wz_in,
    w1_in,
    w2_in,
    x_out,
    total,
    node,
    cot,
    rotation,
    mine,
    land,
    cots,
    rot,
    raw,
    radial,
    gz,
    g1,
    g2,
    hz,
    h1,
    h2,
    wz,
    w1,
    w2,
    fb,
    y,
    back_mine,
    back_land,
    pieces,
    near,
    passing,
    relay,
    fin,
    halo_sent,
    halo_got,
    chan_sent,
    chan_got,
    near_sent,
    near_got,
    far_sent,
    relay_got,
    fin_got,
    back_sent,
    back_got,
    load_got,
    weight_got,
):
    parts, halo, rows_x = land.shape
    groups = cots.shape[0]
    atoms = node.shape[1]
    slots = parts * halo
    edges = rotation.shape[1]
    blocks = edges // LANES
    width = rows_x // 49
    channels = width * groups
    share = channels // parts
    me = lax.axis_index("atoms")
    group = lax.axis_index("chan")
    line, side = me // 2, lax.rem(me, 2)
    other = line * 2 + 1 - side
    mate = line + 1 - 2 * lax.rem(line, 2)
    inner = (line + 1) // 2 == 1
    across, core = group // 2, lax.rem(group, 2)

    def flipped(code):
        a = 1 - across if code >= 2 else across
        c = 1 - core if code % 2 else core
        return a * 2 + c

    far_pair = 1 - line // 2
    distant = (far_pair + across) % 2
    first_far, second_far = far_pair * 2 + core, far_pair * 2 + 1 - core
    steps = [
        mate * distant + first_far * (1 - distant),
        first_far * distant + second_far * (1 - distant),
        second_far * distant + mate * (1 - distant),
        line,
    ]

    def push(src, dst, sent, got, where):
        return pltpu.make_async_remote_copy(
            src_ref=src,
            dst_ref=dst,
            send_sem=sent,
            recv_sem=got,
            device_id=where,
            device_id_type=MESH,
        )

    loads = []
    for slot, (src, dst) in enumerate(((node_in, node), (cot_in, cot), (rotation_in, rotation))):
        copy = pltpu.make_async_copy(src, dst, load_got.at[slot])
        copy.start()
        loads.append(copy)
    barrier = pltpu.get_barrier_semaphore()
    for k in range(1, parts):
        pl.semaphore_signal(
            barrier, inc=1, device_id={"atoms": lax.rem(me + k, parts)}, device_id_type=MESH
        )
    for code in (1, 2):
        pl.semaphore_signal(
            barrier, inc=1, device_id={"chan": flipped(code)}, device_id_type=MESH
        )
    sends = jnp.concatenate([column(sends_in[p : p + 1, :]) for p in range(parts)], axis=0)
    sends = sends.astype(jnp.int32)
    loads[0].wait()
    picked = dot(onehot_cols(sends, atoms), node[...], NT).astype(BF)
    for p in range(parts):
        mine[p] = picked[p * halo : (p + 1) * halo, :]
    pl.semaphore_wait(barrier, parts + 1)

    halo_copies = []
    for k in range(1, parts):
        peer = lax.rem(me + k, parts)
        copy = push(
            mine.at[peer], land.at[me], halo_sent.at[k], halo_got.at[k], {"atoms": peer}
        )
        copy.start()
        halo_copies.append(copy)
    eye = onehot_cols(lax.broadcasted_iota(jnp.int32, (atoms, 1), 0), atoms)
    loads[1].wait()
    cots[group] = dot(eye, cot[...], NT).astype(BF)

    def chan_copy(slot, which, code):
        return push(
            cots.at[which],
            cots.at[which],
            chan_sent.at[slot],
            chan_got.at[slot],
            {"chan": flipped(code)},
        )

    chan_copies = [chan_copy(0, group, 1), chan_copy(1, group, 2)]
    for copy in chan_copies:
        copy.start()
    land[me] = mine[me]
    weight_loads = []
    for src, dst in ((wz_in, wz), (w1_in, w1), (w2_in, w2)):
        lead = (slice(None),) * (len(src.shape) - 4)
        for j in range(src.shape[-3]):
            copy = pltpu.make_async_copy(
                src.at[lead + (slice(None), j)],
                dst.at[lead + (slice(None), slice(None), pl.ds(j * channels, channels))],
                weight_got.at[len(weight_loads)],
            )
            copy.start()
            weight_loads.append(copy)

    loads[2].wait()
    rot[...] = rotation[...].astype(F32)
    ids = source[...]
    own = onehot(ids, atoms)
    remote = onehot(ids - atoms, slots)
    order = lax.broadcasted_iota(jnp.int32, (halo, 1), 0)
    valid = jnp.concatenate(
        [(order < counts_in[:, p : p + 1]).astype(F32) for p in range(parts)], axis=0
    )
    usable = jnp.sum(remote.astype(F32) * valid, axis=0, keepdims=True)
    usable = jnp.where(ids < atoms, 1.0, usable)
    place = lax.broadcasted_iota(jnp.int32, (1, edges), 1)
    radial[...] = jnp.where(place < count[...], envelope[...] * usable, 0.0)
    to = onehot(target[...], atoms)

    g12 = {1: g1, 2: g2}
    h12 = {1: h1, 2: h2}

    def frame_grad(q):
        raw[...] = dot(cots[q], to, TN)

        def one(block, carry):
            e = cols(block)
            scale = radial[:, e]

            def put(degree, m, value):
                value = (value * scale).astype(BF)
                o = abs(m)
                row = pl.ds(
                    pl.multiple_of((degree - o) * channels + q * width, width), width
                )
                if o == 0:
                    gz[row, e] = value
                else:
                    g12[o][row, cols(block, 0 if m > 0 else edges)] = value

            rotate_in(rot, raw, block, width, put)
            return carry

        lax.fori_loop(0, blocks, one, 0)

    def one_h(block, carry):
        e = cols(block)
        later = cols(block, edges)

        def put(degree, m, value):
            value = value.astype(BF)
            o = abs(m)
            first = (degree - o) * width
            second = (7 - o + degree - o) * width
            if o == 0:
                hz[pl.ds(first, width), e] = value
            elif m > 0:
                h12[o][pl.ds(first, width), e] = value
                h12[o][pl.ds(second, width), later] = value
            else:
                h12[o][pl.ds(first, width), later] = value
                h12[o][pl.ds(second, width), e] = -value

        rotate_in(rot, raw, block, width, put)
        return carry

    spans = []
    base = 0
    for count_l, h in ((7, hz), (6, h1), (5, h2)):
        rows = h.shape[0] // LANES * count_l * share
        spans.append(pl.ds(base, rows))
        base += rows
    near_copies = {}

    def weight_piece(k):
        q = steps[k]
        for c, (count_l, g, h) in enumerate(((7, gz, hz), (6, g1, h1), (5, g2, h2))):
            left = jnp.concatenate(
                [
                    g[pl.ds(pl.multiple_of(l * channels + q * width, width), width), :]
                    for l in range(count_l)
                ],
                axis=0,
            )
            part = dot(left, h[...], NT).astype(BF)
            base = spans[c].start
            for tile in range(h.shape[0] // LANES):
                for degree in range(count_l):
                    start = base + (tile * count_l + degree) * share
                    for half in range(2):
                        row = degree * width + half * share
                        pieces[k, half, start : start + share, :] = part[
                            row : row + share, tile * LANES : (tile + 1) * LANES
                        ]
            copy = push(
                pieces.at[k, 1 - side, spans[c]],
                near.at[k, spans[c]],
                near_sent.at[k, c],
                near_got.at[k, c],
                {"atoms": other},
            )
            copy.start()
            near_copies[k, c] = copy

    def relay_copy(k, c):
        return push(
            passing.at[k, spans[c]],
            relay.at[k, spans[c]],
            far_sent.at[k, c],
            relay_got.at[k, c],
            {"atoms": mate * 2 + side},
        )

    def fin_copy(k, c, slot, q):
        return push(
            passing.at[k, spans[c]],
            fin.at[slot, spans[c]],
            far_sent.at[k, c],
            fin_got.at[slot, c],
            {"atoms": q * 2 + side},
        )

    def summed(k, c):
        return pieces[k, side, spans[c]].astype(F32) + near[k, spans[c]].astype(F32)

    def pass_on(k, c):
        near_copies[k, c].wait_recv()
        if k == groups - 1:
            total[spans[c], :] = summed(k, c)
            return

        @pl.when(steps[k] == mate)
        def direct():
            passing[k, spans[c], :] = summed(k, c).astype(BF)
            fin_copy(k, c, 0, mate).start()

        @pl.when((steps[k] != mate) & jnp.logical_not(inner))
        def hand():
            passing[k, spans[c], :] = summed(k, c).astype(BF)
            relay_copy(k, c).start()

    def relay_on(k, c):
        @pl.when((steps[k] != mate) & inner)
        def join():
            relay_copy(k, c).wait_recv()
            value = summed(k, c) + relay[k, spans[c]].astype(F32)
            passing[k, spans[c], :] = value.astype(BF)
            fin_copy(k, c, 1, steps[k]).start()

    frame_grad(group)
    chan_copies[0].wait_recv()
    frame_grad(flipped(1))
    for copy in halo_copies:
        copy.wait_recv()
    hz[...] = jnp.zeros_like(hz)
    h2[...] = jnp.zeros_like(h2)
    table = land[...].astype(F32).reshape(slots, rows_x).astype(BF)
    raw[...] = dot(node[...], own, NN) + dot(table, remote, TN)
    lax.fori_loop(0, blocks, one_h, 0)
    weight_piece(0)

    chan_copies[1].wait_recv()
    chan_copies.append(chan_copy(2, flipped(2), 1))
    chan_copies[2].start()
    frame_grad(flipped(2))
    weight_piece(1)
    chan_copies[2].wait_recv()
    frame_grad(flipped(3))
    weight_piece(2)
    weight_piece(3)

    for copy in weight_loads:
        copy.wait()
    for c in range(3):
        pass_on(0, c)

    fb[pl.ds(0, 7 * width), :] = dot(wz[...].reshape(7 * width, 7 * channels), gz[...], NN)
    start = 7 * width
    for count_l, w, g in ((6, w1, g1), (5, w2, g2)):
        rows = count_l * width
        real = dot(w[0].reshape(rows, count_l * channels), g[...], NN)
        imag = dot(w[1].reshape(rows, count_l * channels), g[...], NN)
        fb[pl.ds(start, rows), :] = real[:, :edges] + imag[:, edges:]
        fb[pl.ds(start + rows, rows), :] = real[:, edges:] - imag[:, :edges]
        start += 2 * rows

    def one_back(block, carry):
        rotate_out(rot, fb, block, width, y)
        return carry

    lax.fori_loop(0, blocks, one_back, 0)
    for c in range(3):
        pass_on(1, c)
    terms = dot(remote, y[...], NT).astype(BF)
    for p in range(parts):
        back_mine[p] = terms[p * halo : (p + 1) * halo, :]
    back_copies = []
    for k in range(1, parts):
        peer = lax.rem(me + k, parts)
        copy = push(
            back_mine.at[peer],
            back_land.at[me],
            back_sent.at[k],
            back_got.at[k],
            {"atoms": peer},
        )
        copy.start()
        back_copies.append(copy)
    back_land[me] = back_mine[me]
    for c in range(3):
        relay_on(0, c)
    x_out[...] = dot(y[...], own, NT)
    for c in range(3):
        pass_on(2, c)
    for c in range(3):
        relay_on(1, c)
    for c in range(3):
        relay_on(2, c)
        pass_on(3, c)
    for copy in back_copies:
        copy.wait_recv()
    returned = back_land[...].astype(F32).reshape(slots, rows_x).astype(BF)
    x_out[...] += dot(returned, onehot_cols(sends, atoms), TN)

    for c in range(3):
        value = total[spans[c], :]
        for slot in range(2):
            fin_copy(0, c, slot, mate).wait_recv()
            value = value + fin[slot, spans[c]].astype(F32)
        total[spans[c], :] = value * factor

    for copy in halo_copies + chan_copies + list(near_copies.values()) + back_copies:
        copy.wait_send()
    for k in range(groups - 1):
        for c in range(3):
            relay_copy(k, c).wait_send()


def write_kernel(x, total, x_out, dz_out, d1_out, d2_out):
    x_out[...] = x[...]
    base = 0
    for c, out in enumerate((dz_out, d1_out, d2_out)):
        share, width = out.shape[-2:]
        count_l = 7 - c
        high = count_l if c == 0 else 2 * count_l
        for i in range(high):
            tile, lane = divmod(i * width, LANES)
            for j in range(count_l):
                row = base + (tile * count_l + j) * share
                cut = total[row : row + share, lane : lane + width]
                if c == 0:
                    out[i, j] = cut
                else:
                    out[i // count_l, i % count_l, j] = cut
        base += -(-high * width // LANES) * count_l * share


def call(kernel, outs, scratch=(), flops=10**8, collective=None, specs=None):
    if collective is None:
        params = pltpu.CompilerParams(vmem_limit_bytes=VMEM_LIMIT)
    else:
        params = pltpu.CompilerParams(
            vmem_limit_bytes=VMEM_LIMIT, collective_id=collective, has_side_effects=True
        )
    extra = {} if specs is None else {"in_specs": specs}
    return pl.pallas_call(
        kernel,
        out_shape=outs,
        **extra,
        scratch_shapes=list(scratch),
        compiler_params=params,
        cost_estimate=pl.CostEstimate(
            flops=flops, bytes_accessed=8 * 10**6, transcendentals=0
        ),
    )


def on_device(
    node_x,
    cotangent,
    rotation,
    envelope,
    source,
    target,
    edge_count,
    send_index,
    halo_count,
    weight_zero,
    weight_one,
    weight_two,
):
    parts = lax.axis_size("atoms")
    groups = lax.axis_size("chan")
    width = node_x.shape[1]
    channels = width * groups
    atoms = node_x.shape[2]
    halo = send_index.shape[2]
    edges = source.shape[0]
    slots = parts * halo
    rows = 49 * width
    share = channels // parts
    fast = parts == 8 and groups == 4 and share % 16 == 0 and width == 2 * share
    sds = jax.ShapeDtypeStruct

    node = node_x.reshape(rows, atoms)
    cot = cotangent.reshape(rows, atoms)
    factor = 1.0 / math.sqrt(edges * parts)
    src = source.reshape(1, edges)
    tgt = target.reshape(1, edges)
    pad = lambda n: -(-n // LANES) * LANES
    lz, l1, l2 = pad(7 * width), pad(12 * width), pad(10 * width)

    if fast:
        height = (7 * lz + 6 * l1 + 5 * l2) // LANES * share
        vmem = pltpu.VMEM
        dma = pltpu.SemaphoreType.DMA
        grad_x, summed = call(
            functools.partial(whole_kernel, factor),
            (sds((rows, atoms), F32), sds((height, LANES), F32)),
            (
                vmem((rows, atoms), BF),
                vmem((rows, atoms), BF),
                vmem((235, edges), BF),
                vmem((parts, halo, rows), BF),
                vmem((parts, halo, rows), BF),
                vmem((groups, atoms, rows), BF),
                vmem((235, edges), F32),
                vmem((rows, edges), F32),
                vmem((1, edges), F32),
                vmem((7 * channels, edges), BF),
                vmem((6 * channels, 2 * edges), BF),
                vmem((5 * channels, 2 * edges), BF),
                vmem((lz, edges), BF),
                vmem((l1, 2 * edges), BF),
                vmem((l2, 2 * edges), BF),
                vmem((7, width, 7 * channels), BF),
                vmem((2, 6, width, 6 * channels), BF),
                vmem((2, 5, width, 5 * channels), BF),
                vmem((29 * width, edges), F32),
                vmem((rows, edges), BF),
                vmem((parts, halo, rows), BF),
                vmem((parts, halo, rows), BF),
                vmem((groups, 2, height, LANES), BF),
                vmem((groups, height, LANES), BF),
                vmem((groups, height, LANES), BF),
                vmem((groups, height, LANES), BF),
                vmem((2, height, LANES), BF),
                dma((parts,)),
                dma((parts,)),
                dma((3,)),
                dma((3,)),
                dma((groups, 3)),
                dma((groups, 3)),
                dma((groups, 3)),
                dma((groups, 3)),
                dma((2, 3)),
                dma((parts,)),
                dma((parts,)),
                dma((3,)),
                dma((18,)),
            ),
            flops=10**10,
            collective=0,
            specs=[
                pl.BlockSpec(memory_space=pltpu.HBM if far else pltpu.VMEM)
                for far in (0, 1, 1, 1, 0, 0, 0, 0, 0, 1, 1, 1)
            ],
        )(
            send_index[0],
            node,
            cot,
            rotation,
            envelope.reshape(1, edges),
            src,
            tgt,
            edge_count.reshape(1, 1),
            halo_count.reshape(1, parts),
            weight_zero.transpose(0, 2, 1, 3),
            weight_one.transpose(0, 1, 3, 2, 4),
            weight_two.transpose(0, 1, 3, 2, 4),
        )
        grad_x, dz, d1, d2 = call(
            write_kernel,
            (
                sds((rows, atoms), F32),
                sds((7, 7, share, width), F32),
                sds((2, 6, 6, share, width), F32),
                sds((2, 5, 5, share, width), F32),
            ),
        )(grad_x, summed)
        return (
            grad_x.reshape(49, width, atoms),
            dz.transpose(0, 3, 1, 2),
            d1.transpose(0, 1, 4, 2, 3),
            d2.transpose(0, 1, 4, 2, 3),
        )

    sends = send_index.reshape(slots, 1)
    send_rows, cot_rows = call(
        prep_kernel, (sds((slots, rows), BF), sds((atoms, rows), BF))
    )(sends, node, cot)
    recv = lax.all_to_all(send_rows, "atoms", split_axis=0, concat_axis=0, tiled=True)
    cots = lax.all_gather(cot_rows, "chan", axis=0, tiled=False)
    valid = (
        jnp.arange(halo, dtype=jnp.int32)[None, :] < halo_count[:, 0][:, None]
    ).astype(F32).reshape(slots, 1)
    g_shapes = (
        sds((7 * channels, edges), BF),
        sds((6 * channels, 2 * edges), BF),
        sds((5 * channels, 2 * edges), BF),
    )
    d_shapes = (
        sds((7 * channels, lz), F32),
        sds((6 * channels, l1), F32),
        sds((5 * channels, l2), F32),
    )
    made = call(
        frame_kernel,
        g_shapes + d_shapes,
        (
            pltpu.VMEM((235, edges), F32),
            pltpu.VMEM((rows, edges), F32),
            pltpu.VMEM((1, edges), F32),
            pltpu.VMEM((lz, edges), BF),
            pltpu.VMEM((l1, 2 * edges), BF),
            pltpu.VMEM((l2, 2 * edges), BF),
        ),
        flops=10**10,
    )(
        node,
        recv,
        cots,
        rotation,
        envelope.reshape(1, edges),
        src,
        tgt,
        edge_count.reshape(1, 1),
        valid,
    )
    gz, g1, g2 = made[:3]
    own, halo_rows = call(
        back_kernel,
        (sds((rows, atoms), F32), sds((slots, rows), BF)),
        (
            pltpu.VMEM((235, edges), F32),
            pltpu.VMEM((29 * width, edges), F32),
            pltpu.VMEM((rows, edges), BF),
        ),
        flops=10**10,
    )(
        gz,
        g1,
        g2,
        weight_zero.reshape(7 * width, 7 * channels),
        weight_one.reshape(12 * width, 6 * channels),
        weight_two.reshape(10 * width, 5 * channels),
        rotation,
        src,
    )
    back = lax.all_to_all(halo_rows, "atoms", split_axis=0, concat_axis=0, tiled=True)
    grad_x = call(join_kernel, sds((rows, atoms), F32))(own, back, sends)

    dz = made[3][:, : 7 * width].reshape(7, channels, 7, width)
    d1 = made[4].reshape(6, channels, 2, 6, width)
    d2 = made[5][:, : 10 * width].reshape(5, channels, 2, 5, width)
    dz = lax.psum_scatter(dz, "atoms", scatter_dimension=1, tiled=True)
    d1 = lax.psum_scatter(d1, "atoms", scatter_dimension=1, tiled=True)
    d2 = lax.psum_scatter(d2, "atoms", scatter_dimension=1, tiled=True)
    return (
        grad_x.reshape(49, width, atoms),
        dz.transpose(2, 3, 0, 1) * factor,
        d1.transpose(2, 3, 4, 0, 1) * factor,
        d2.transpose(2, 3, 4, 0, 1) * factor,
    )


def solution(mesh):
    in_specs = (
        P(None, "chan", "atoms"),
        P(None, "chan", "atoms"),
        P(None, "atoms"),
        P("atoms"),
        P("atoms"),
        P("atoms"),
        P("atoms"),
        P("atoms", None, None),
        P(None, "atoms"),
        P(None, "chan", None, None),
        P(None, None, "chan", None, None),
        P(None, None, "chan", None, None),
    )
    out_specs = (
        P(None, "chan", "atoms"),
        P(None, "chan", None, "atoms"),
        P(None, None, "chan", None, "atoms"),
        P(None, None, "chan", None, "atoms"),
    )
    return jax.shard_map(
        on_device, mesh=mesh, in_specs=in_specs, out_specs=out_specs, check_vma=False
    )
```

```python
import functools
import math

import jax
import jax.numpy as jnp
from jax import lax
from jax.experimental import pallas as pl
from jax.experimental.pallas import tpu as pltpu
from jax.sharding import PartitionSpec as P

LANES = 128
BF = jnp.bfloat16
F32 = jnp.float32
VMEM_LIMIT = 56 * 1024 * 1024
MESH = pl.DeviceIdType.MESH


def dot(a, b, dims):
    return lax.dot_general(a, b, (dims, ((), ())), preferred_element_type=F32)


NN = ((1,), (0,))
NT = ((1,), (1,))
TN = ((0,), (0,))


def degrees():
    offset = 0
    for degree in range(7):
        reach = min(degree, 2)
        yield degree, reach, offset
        offset += (2 * reach + 1) * (2 * degree + 1)


def cols(block, base=0):
    return pl.ds(pl.multiple_of(base + block * LANES, LANES), LANES)


def rotate_in(rot, raw, block, width, put):
    e = cols(block)
    for degree, reach, offset in degrees():
        breadth = 2 * degree + 1
        acc = [None] * (2 * reach + 1)
        for k in range(breadth):
            v = raw[pl.ds((degree * degree + k) * width, width), e]
            for r in range(2 * reach + 1):
                term = rot[pl.ds(offset + r * breadth + k, 1), e] * v
                acc[r] = term if acc[r] is None else acc[r] + term
        for r in range(2 * reach + 1):
            put(degree, r - reach, acc[r])


def rotate_out(rot, framed, block, width, out):
    e = cols(block)
    spots = {}
    for i, pair in enumerate(frame_pairs()):
        spots[pair] = i
    for degree, reach, offset in degrees():
        breadth = 2 * degree + 1
        u = [
            framed[pl.ds(spots[degree, m] * width, width), e]
            for m in range(-reach, reach + 1)
        ]
        for k in range(breadth):
            acc = None
            for r in range(2 * reach + 1):
                term = rot[pl.ds(offset + r * breadth + k, 1), e] * u[r]
                acc = term if acc is None else acc + term
            out[pl.ds((degree * degree + k) * width, width), e] = acc.astype(BF)


def frame_pairs():
    listing = [(degree, 0) for degree in range(7)]
    for order in (1, 2):
        listing = listing + [(degree, order) for degree in range(order, 7)]
        listing = listing + [(degree, -order) for degree in range(order, 7)]
    return listing


def onehot(ids, rows):
    return (lax.broadcasted_iota(jnp.int32, (rows, ids.shape[1]), 0) == ids).astype(BF)


def onehot_cols(ids, columns):
    return (lax.broadcasted_iota(jnp.int32, (ids.shape[0], columns), 1) == ids).astype(BF)


def prep_kernel(sends, node, cot, send_out, cot_out):
    atoms = node.shape[1]
    send_out[...] = dot(onehot_cols(sends[...], atoms), node[...], NT).astype(BF)
    eye = onehot_cols(lax.broadcasted_iota(jnp.int32, (atoms, 1), 0), atoms)
    cot_out[...] = dot(eye, cot[...], NT).astype(BF)


def frame_kernel(
    node,
    recv,
    cot,
    rotation,
    envelope,
    source,
    target,
    count,
    valid,
    gz,
    g1,
    g2,
    dz_out,
    d1_out,
    d2_out,
    rot,
    raw,
    radial,
    hz,
    h1,
    h2,
):
    atoms = node.shape[1]
    slots = recv.shape[0]
    edges = rotation.shape[1]
    blocks = edges // LANES
    groups = cot.shape[0]
    width = node.shape[0] // 49
    channels = gz.shape[0] // 7
    g12 = {1: g1, 2: g2}
    h12 = {1: h1, 2: h2}

    rot[...] = rotation[...].astype(F32)
    ids = source[...]
    own = onehot(ids, atoms)
    halo = onehot(ids - atoms, slots)
    usable = jnp.sum(halo.astype(F32) * valid[...], axis=0, keepdims=True)
    usable = jnp.where(ids < atoms, 1.0, usable)
    place = lax.broadcasted_iota(jnp.int32, (1, edges), 1)
    radial[...] = jnp.where(place < count[...], envelope[...] * usable, 0.0)
    to = onehot(target[...], atoms)

    def group(q, carry):
        raw[...] = dot(cot[q], to, TN)

        def one(block, carry):
            e = cols(block)
            scale = radial[:, e]

            def put(degree, m, value):
                value = (value * scale).astype(BF)
                order = abs(m)
                row = pl.ds(
                    pl.multiple_of((degree - order) * channels + q * width, width), width
                )
                if order == 0:
                    gz[row, e] = value
                else:
                    g12[order][row, cols(block, 0 if m > 0 else edges)] = value

            rotate_in(rot, raw, block, width, put)
            return carry

        return lax.fori_loop(0, blocks, one, carry)

    lax.fori_loop(0, groups, group, 0)

    raw[...] = dot(node[...], own, NN) + dot(recv[...], halo, TN)
    hz[...] = jnp.zeros_like(hz)
    h2[...] = jnp.zeros_like(h2)

    def one_h(block, carry):
        e = cols(block)
        later = cols(block, edges)

        def put(degree, m, value):
            value = value.astype(BF)
            order = abs(m)
            first = (degree - order) * width
            second = (7 - order + degree - order) * width
            if order == 0:
                hz[pl.ds(first, width), e] = value
            elif m > 0:
                h12[order][pl.ds(first, width), e] = value
                h12[order][pl.ds(second, width), later] = value
            else:
                h12[order][pl.ds(first, width), later] = value
                h12[order][pl.ds(second, width), e] = -value

        rotate_in(rot, raw, block, width, put)
        return carry

    lax.fori_loop(0, blocks, one_h, 0)

    dz_out[...] = dot(gz[...], hz[...], NT)
    d1_out[...] = dot(g1[...], h1[...], NT)
    d2_out[...] = dot(g2[...], h2[...], NT)


def back_kernel(gz, g1, g2, wz, w1, w2, rotation, source, own_out, halo_out, rot, fb, y):
    edges = rotation.shape[1]
    blocks = edges // LANES
    atoms = own_out.shape[1]
    slots = halo_out.shape[0]
    width = wz.shape[0] // 7
    rot[...] = rotation[...].astype(F32)
    fb[pl.ds(0, 7 * width), :] = dot(wz[...], gz[...], NN)
    start = 7 * width
    for count_l, w, g in ((6, w1, g1), (5, w2, g2)):
        rows = count_l * width
        real = dot(w[pl.ds(0, rows), :], g[...], NN)
        imag = dot(w[pl.ds(rows, rows), :], g[...], NN)
        fb[pl.ds(start, rows), :] = real[:, :edges] + imag[:, edges:]
        fb[pl.ds(start + rows, rows), :] = real[:, edges:] - imag[:, :edges]
        start += 2 * rows

    def one(block, carry):
        rotate_out(rot, fb, block, width, y)
        return carry

    lax.fori_loop(0, blocks, one, 0)
    ids = source[...]
    own_out[...] = dot(y[...], onehot(ids, atoms), NT)
    halo_out[...] = dot(onehot(ids - atoms, slots), y[...], NT).astype(BF)


def join_kernel(own, back, sends, out):
    out[...] = own[...] + dot(back[...], onehot_cols(sends[...], own.shape[1]), TN)


def column(row):
    n = row.shape[1]
    diag = lax.broadcasted_iota(jnp.int32, (n, n), 0) == lax.broadcasted_iota(
        jnp.int32, (n, n), 1
    )
    spread = jnp.where(diag, jnp.broadcast_to(row.astype(F32), (n, n)), 0.0)
    return jnp.sum(spread, axis=1, keepdims=True)


def whole_kernel(
    factor,
    sends_in,
    node_in,
    cot_in,
    rotation_in,
    envelope,
    source,
    target,
    count,
    counts_in,
    wz_in,
    w1_in,
    w2_in,
    x_out,
    total,
    node,
    cot,
    rotation,
    mine,
    land,
    cots,
    rot,
    raw,
    radial,
    gz,
    g1,
    g2,
    hz,
    h1,
    h2,
    wz,
    w1,
    w2,
    fb,
    y,
    back_mine,
    back_land,
    pieces,
    near,
    passing,
    relay,
    fin,
    halo_sent,
    halo_got,
    chan_sent,
    chan_got,
    near_sent,
    near_got,
    far_sent,
    relay_got,
    fin_got,
    back_sent,
    back_got,
    load_got,
    weight_got,
):
    parts, halo, rows_x = land.shape
    groups = cots.shape[0]
    atoms = node.shape[1]
    slots = parts * halo
    edges = rotation.shape[1]
    blocks = edges // LANES
    width = rows_x // 49
    channels = width * groups
    share = channels // parts
    me = lax.axis_index("atoms")
    group = lax.axis_index("chan")
    line, side = me // 2, lax.rem(me, 2)
    other = line * 2 + 1 - side
    mate = line + 1 - 2 * lax.rem(line, 2)
    inner = (line + 1) // 2 == 1
    across, core = group // 2, lax.rem(group, 2)

    def flipped(code):
        a = 1 - across if code >= 2 else across
        c = 1 - core if code % 2 else core
        return a * 2 + c

    far_pair = 1 - line // 2
    distant = (far_pair + across) % 2
    first_far, second_far = far_pair * 2 + core, far_pair * 2 + 1 - core
    steps = [
        mate * distant + first_far * (1 - distant),
        first_far * distant + second_far * (1 - distant),
        second_far * distant + mate * (1 - distant),
        line,
    ]

    def push(src, dst, sent, got, where):
        return pltpu.make_async_remote_copy(
            src_ref=src,
            dst_ref=dst,
            send_sem=sent,
            recv_sem=got,
            device_id=where,
            device_id_type=MESH,
        )

    loads = []
    for slot, (src, dst) in enumerate(((node_in, node), (cot_in, cot), (rotation_in, rotation))):
        copy = pltpu.make_async_copy(src, dst, load_got.at[slot])
        copy.start()
        loads.append(copy)
    barrier = pltpu.get_barrier_semaphore()
    for k in range(1, parts):
        pl.semaphore_signal(
            barrier, inc=1, device_id={"atoms": lax.rem(me + k, parts)}, device_id_type=MESH
        )
    for code in (1, 2):
        pl.semaphore_signal(
            barrier, inc=1, device_id={"chan": flipped(code)}, device_id_type=MESH
        )
    sends = jnp.concatenate([column(sends_in[p : p + 1, :]) for p in range(parts)], axis=0)
    sends = sends.astype(jnp.int32)
    loads[0].wait()
    picked = dot(onehot_cols(sends, atoms), node[...], NT).astype(BF)
    for p in range(parts):
        mine[p] = picked[p * halo : (p + 1) * halo, :]
    pl.semaphore_wait(barrier, parts + 1)

    halo_copies = []
    for k in range(1, parts):
        peer = lax.rem(me + k, parts)
        copy = push(
            mine.at[peer], land.at[me], halo_sent.at[k], halo_got.at[k], {"atoms": peer}
        )
        copy.start()
        halo_copies.append(copy)
    eye = onehot_cols(lax.broadcasted_iota(jnp.int32, (atoms, 1), 0), atoms)
    loads[1].wait()
    cots[group] = dot(eye, cot[...], NT).astype(BF)

    def chan_copy(slot, which, code):
        return push(
            cots.at[which],
            cots.at[which],
            chan_sent.at[slot],
            chan_got.at[slot],
            {"chan": flipped(code)},
        )

    chan_copies = [chan_copy(0, group, 1), chan_copy(1, group, 2)]
    for copy in chan_copies:
        copy.start()
    land[me] = mine[me]
    weight_loads = []
    for src, dst in ((wz_in, wz), (w1_in, w1), (w2_in, w2)):
        lead = (slice(None),) * (len(src.shape) - 4)
        for j in range(src.shape[-3]):
            copy = pltpu.make_async_copy(
                src.at[lead + (slice(None), j)],
                dst.at[lead + (slice(None), slice(None), pl.ds(j * channels, channels))],
                weight_got.at[len(weight_loads)],
            )
            copy.start()
            weight_loads.append(copy)

    loads[2].wait()
    rot[...] = rotation[...].astype(F32)
    ids = source[...]
    own = onehot(ids, atoms)
    remote = onehot(ids - atoms, slots)
    order = lax.broadcasted_iota(jnp.int32, (halo, 1), 0)
    valid = jnp.concatenate(
        [(order < counts_in[:, p : p + 1]).astype(F32) for p in range(parts)], axis=0
    )
    usable = jnp.sum(remote.astype(F32) * valid, axis=0, keepdims=True)
    usable = jnp.where(ids < atoms, 1.0, usable)
    place = lax.broadcasted_iota(jnp.int32, (1, edges), 1)
    radial[...] = jnp.where(place < count[...], envelope[...] * usable, 0.0)
    to = onehot(target[...], atoms)

    g12 = {1: g1, 2: g2}
    h12 = {1: h1, 2: h2}

    def frame_grad(q, low=0, high=blocks):
        if low == 0:
            raw[...] = dot(cots[q], to, TN)

        def one(block, carry):
            e = cols(block)
            scale = radial[:, e]

            def put(degree, m, value):
                value = (value * scale).astype(BF)
                o = abs(m)
                row = pl.ds(
                    pl.multiple_of((degree - o) * channels + q * width, width), width
                )
                if o == 0:
                    gz[row, e] = value
                else:
                    g12[o][row, cols(block, 0 if m > 0 else edges)] = value

            rotate_in(rot, raw, block, width, put)
            return carry

        lax.fori_loop(low, high, one, 0)

    def one_h(block, carry):
        e = cols(block)
        later = cols(block, edges)

        def put(degree, m, value):
            value = value.astype(BF)
            o = abs(m)
            first = (degree - o) * width
            spot = 7 - o + degree - o
            if o == 2 and spot >= 8:
                spot = 11 if spot == 8 else 8
            second = spot * width
            if o == 0:
                hz[pl.ds(first, width), e] = value
            elif m > 0:
                h12[o][pl.ds(first, width), e] = value
                h12[o][pl.ds(second, width), later] = value
            else:
                h12[o][pl.ds(first, width), later] = value
                h12[o][pl.ds(second, width), e] = -value

        rotate_in(rot, raw, block, width, put)
        return carry

    spans = []
    base = 0
    for rows in (14 * share, 18 * share, 11 * share):
        spans.append(pl.ds(base, rows))
        base += rows
    near_copies = {}
    lane = lax.broadcasted_iota(jnp.int32, (1, LANES), 1)

    def weight_piece(k):
        q = steps[k]

        def left(g, count_l):
            return jnp.concatenate(
                [
                    g[pl.ds(pl.multiple_of(l * channels + q * width, width), width), :]
                    for l in range(count_l)
                ],
                axis=0,
            )

        def place(start, value):
            value = value.astype(BF)
            for degree in range(value.shape[0] // width):
                for half in range(2):
                    row = degree * width + half * share
                    at = start + degree * share
                    pieces[k, half, at : at + share, :] = value[row : row + share, :]

        left_two = left(g2, 5)
        tail = dot(left_two, h2[pl.ds(2 * LANES, LANES), :], NT)
        part = dot(left(gz, 7), hz[...], NT)
        last = jnp.concatenate([tail, pltpu.roll(tail[: 2 * width], 3 * width, 1)], axis=0)
        place(0, part[:, :LANES])
        place(7 * share, jnp.where(lane < 3 * width, part[:, LANES:], last))
        send_near(k, 0)
        part = dot(left(g1, 6), h1[...], NT)
        for tile in range(3):
            place(spans[1].start + tile * 6 * share, part[:, tile * LANES : (tile + 1) * LANES])
        send_near(k, 1)
        part = dot(left_two, h2[pl.ds(0, 2 * LANES), :], NT)
        for tile in range(2):
            place(spans[2].start + tile * 5 * share, part[:, tile * LANES : (tile + 1) * LANES])
        third = pltpu.roll(tail[3 * width : 4 * width], width, 1)
        fourth = pltpu.roll(tail[4 * width :], 2 * width, 1)
        third = jnp.where(lane < 2 * width, third, fourth)
        place(spans[2].start + 10 * share, jnp.where(lane < width, tail[2 * width : 3 * width], third))
        send_near(k, 2)

    def send_near(k, c):
        copy = push(
            pieces.at[k, 1 - side, spans[c]],
            near.at[k, spans[c]],
            near_sent.at[k, c],
            near_got.at[k, c],
            {"atoms": other},
        )
        copy.start()
        near_copies[k, c] = copy

    def relay_copy(k, c):
        return push(
            passing.at[k, spans[c]],
            relay.at[k, spans[c]],
            far_sent.at[k, c],
            relay_got.at[k, c],
            {"atoms": mate * 2 + side},
        )

    def fin_copy(k, c, slot, q):
        return push(
            passing.at[k, spans[c]],
            fin.at[slot, spans[c]],
            far_sent.at[k, c],
            fin_got.at[slot, c],
            {"atoms": q * 2 + side},
        )

    def summed(k, c):
        return pieces[k, side, spans[c]].astype(F32) + near[k, spans[c]].astype(F32)

    def pass_on(k, c):
        near_copies[k, c].wait_recv()
        if k == groups - 1:
            total[spans[c], :] = summed(k, c)
            return

        @pl.when(steps[k] == mate)
        def direct():
            passing[k, spans[c], :] = summed(k, c).astype(BF)
            fin_copy(k, c, 0, mate).start()

        @pl.when((steps[k] != mate) & jnp.logical_not(inner))
        def hand():
            passing[k, spans[c], :] = summed(k, c).astype(BF)
            relay_copy(k, c).start()

    def relay_on(k, c):
        @pl.when((steps[k] != mate) & inner)
        def join():
            relay_copy(k, c).wait_recv()
            value = summed(k, c) + relay[k, spans[c]].astype(F32)
            passing[k, spans[c], :] = value.astype(BF)
            fin_copy(k, c, 1, steps[k]).start()

    frame_grad(group)
    chan_copies[0].wait_recv()
    frame_grad(flipped(1))
    for copy in halo_copies:
        copy.wait_recv()
    hz[...] = jnp.zeros_like(hz)
    h2[...] = jnp.zeros_like(h2)
    table = land[...].astype(F32).reshape(slots, rows_x).astype(BF)
    raw[...] = dot(node[...], own, NN) + dot(table, remote, TN)
    lax.fori_loop(0, blocks, one_h, 0)
    weight_piece(0)

    chan_copies[1].wait_recv()
    chan_copies.append(chan_copy(2, flipped(2), 1))
    chan_copies[2].start()
    frame_grad(flipped(2))
    weight_piece(1)
    pass_on(0, 0)
    chan_copies[2].wait_recv()
    frame_grad(flipped(3), 0, blocks // 2)
    pass_on(0, 1)
    frame_grad(flipped(3), blocks // 2, blocks)
    pass_on(0, 2)
    weight_piece(2)

    for copy in weight_loads:
        copy.wait()
    fb[pl.ds(0, 7 * width), :] = dot(wz[...].reshape(7 * width, 7 * channels), gz[...], NN)
    pass_on(1, 0)
    start = 7 * width
    for count_l, w, g in ((6, w1, g1), (5, w2, g2)):
        rows = count_l * width
        real = dot(w[0].reshape(rows, count_l * channels), g[...], NN)
        imag = dot(w[1].reshape(rows, count_l * channels), g[...], NN)
        fb[pl.ds(start, rows), :] = real[:, :edges] + imag[:, edges:]
        fb[pl.ds(start + rows, rows), :] = real[:, edges:] - imag[:, :edges]
        start += 2 * rows
    pass_on(1, 1)
    for c in range(2):
        relay_on(0, c)

    def one_back(block, carry):
        rotate_out(rot, fb, block, width, y)
        return carry

    lax.fori_loop(0, blocks, one_back, 0)
    relay_on(0, 2)
    pass_on(1, 2)
    terms = dot(remote, y[...], NT).astype(BF)
    for p in range(parts):
        back_mine[p] = terms[p * halo : (p + 1) * halo, :]
    back_copies = []
    for k in range(1, parts):
        peer = lax.rem(me + k, parts)
        copy = push(
            back_mine.at[peer],
            back_land.at[me],
            back_sent.at[k],
            back_got.at[k],
            {"atoms": peer},
        )
        copy.start()
        back_copies.append(copy)
    weight_piece(3)
    back_land[me] = back_mine[me]
    pass_on(2, 0)
    relay_on(1, 0)
    x_out[...] = dot(y[...], own, NT)
    pass_on(2, 1)
    relay_on(1, 1)
    pass_on(2, 2)
    relay_on(1, 2)
    pass_on(3, 0)
    relay_on(2, 0)
    relay_on(2, 1)
    relay_on(2, 2)
    pass_on(3, 1)
    pass_on(3, 2)
    for copy in back_copies:
        copy.wait_recv()
    returned = back_land[...].astype(F32).reshape(slots, rows_x).astype(BF)
    x_out[...] += dot(returned, onehot_cols(sends, atoms), TN)

    for c in range(3):
        value = total[spans[c], :]
        for slot in range(2):
            fin_copy(0, c, slot, mate).wait_recv()
            value = value + fin[slot, spans[c]].astype(F32)
        total[spans[c], :] = value * factor

    for copy in halo_copies + chan_copies + list(near_copies.values()) + back_copies:
        copy.wait_send()
    for k in range(groups - 1):
        for c in range(3):
            relay_copy(k, c).wait_send()


def write_kernel(x, total, x_out, dz_out, d1_out, d2_out):
    x_out[...] = x[...]
    share, width = dz_out.shape[-2:]

    def cut(slot, spot):
        return total[slot * share : (slot + 1) * share, spot * width : (spot + 1) * width]

    for i in range(7):
        tile, spot = divmod(i, 4)
        for j in range(7):
            dz_out[i, j] = cut(tile * 7 + j, spot)
    for i in range(12):
        tile, spot = divmod(i, 4)
        for j in range(6):
            d1_out[i // 6, i % 6, j] = cut(14 + tile * 6 + j, spot)
    for i in range(10):
        tile, spot = divmod(i, 4)
        for j in range(5):
            if i < 8:
                where = (32 + tile * 5 + j, spot)
            elif i == 8:
                where = (7 + j, 3)
            else:
                where = (12 + j, 3) if j < 2 else (42, j - 2)
            d2_out[i // 5, i % 5, j] = cut(*where)


def call(kernel, outs, scratch=(), flops=10**8, collective=None, specs=None):
    if collective is None:
        params = pltpu.CompilerParams(vmem_limit_bytes=VMEM_LIMIT)
    else:
        params = pltpu.CompilerParams(
            vmem_limit_bytes=VMEM_LIMIT, collective_id=collective, has_side_effects=True
        )
    extra = {} if specs is None else {"in_specs": specs}
    return pl.pallas_call(
        kernel,
        out_shape=outs,
        **extra,
        scratch_shapes=list(scratch),
        compiler_params=params,
        cost_estimate=pl.CostEstimate(
            flops=flops, bytes_accessed=8 * 10**6, transcendentals=0
        ),
    )


def on_device(
    node_x,
    cotangent,
    rotation,
    envelope,
    source,
    target,
    edge_count,
    send_index,
    halo_count,
    weight_zero,
    weight_one,
    weight_two,
):
    parts = lax.axis_size("atoms")
    groups = lax.axis_size("chan")
    width = node_x.shape[1]
    channels = width * groups
    atoms = node_x.shape[2]
    halo = send_index.shape[2]
    edges = source.shape[0]
    slots = parts * halo
    rows = 49 * width
    share = channels // parts
    fast = parts == 8 and groups == 4 and share % 16 == 0 and width == 2 * share
    sds = jax.ShapeDtypeStruct

    node = node_x.reshape(rows, atoms)
    cot = cotangent.reshape(rows, atoms)
    factor = 1.0 / math.sqrt(edges * parts)
    src = source.reshape(1, edges)
    tgt = target.reshape(1, edges)
    pad = lambda n: -(-n // LANES) * LANES
    lz, l1, l2 = pad(7 * width), pad(12 * width), pad(10 * width)

    if fast:
        height = 43 * share
        vmem = pltpu.VMEM
        dma = pltpu.SemaphoreType.DMA
        grad_x, summed = call(
            functools.partial(whole_kernel, factor),
            (sds((rows, atoms), F32), sds((height, LANES), F32)),
            (
                vmem((rows, atoms), BF),
                vmem((rows, atoms), BF),
                vmem((235, edges), BF),
                vmem((parts, halo, rows), BF),
                vmem((parts, halo, rows), BF),
                vmem((groups, atoms, rows), BF),
                vmem((235, edges), F32),
                vmem((rows, edges), F32),
                vmem((1, edges), F32),
                vmem((7 * channels, edges), BF),
                vmem((6 * channels, 2 * edges), BF),
                vmem((5 * channels, 2 * edges), BF),
                vmem((lz, edges), BF),
                vmem((l1, 2 * edges), BF),
                vmem((l2, 2 * edges), BF),
                vmem((7, width, 7 * channels), BF),
                vmem((2, 6, width, 6 * channels), BF),
                vmem((2, 5, width, 5 * channels), BF),
                vmem((29 * width, edges), F32),
                vmem((rows, edges), BF),
                vmem((parts, halo, rows), BF),
                vmem((parts, halo, rows), BF),
                vmem((groups, 2, height, LANES), BF),
                vmem((groups, height, LANES), BF),
                vmem((groups, height, LANES), BF),
                vmem((groups, height, LANES), BF),
                vmem((2, height, LANES), BF),
                dma((parts,)),
                dma((parts,)),
                dma((3,)),
                dma((3,)),
                dma((groups, 3)),
                dma((groups, 3)),
                dma((groups, 3)),
                dma((groups, 3)),
                dma((2, 3)),
                dma((parts,)),
                dma((parts,)),
                dma((3,)),
                dma((18,)),
            ),
            flops=10**10,
            collective=0,
            specs=[
                pl.BlockSpec(memory_space=pltpu.HBM if far else pltpu.VMEM)
                for far in (0, 1, 1, 1, 0, 0, 0, 0, 0, 1, 1, 1)
            ],
        )(
            send_index[0],
            node,
            cot,
            rotation,
            envelope.reshape(1, edges),
            src,
            tgt,
            edge_count.reshape(1, 1),
            halo_count.reshape(1, parts),
            weight_zero.transpose(0, 2, 1, 3),
            weight_one.transpose(0, 1, 3, 2, 4),
            weight_two.transpose(0, 1, 3, 2, 4),
        )
        grad_x, dz, d1, d2 = call(
            write_kernel,
            (
                sds((rows, atoms), F32),
                sds((7, 7, share, width), F32),
                sds((2, 6, 6, share, width), F32),
                sds((2, 5, 5, share, width), F32),
            ),
        )(grad_x, summed)
        return (
            grad_x.reshape(49, width, atoms),
            dz.transpose(0, 3, 1, 2),
            d1.transpose(0, 1, 4, 2, 3),
            d2.transpose(0, 1, 4, 2, 3),
        )

    sends = send_index.reshape(slots, 1)
    send_rows, cot_rows = call(
        prep_kernel, (sds((slots, rows), BF), sds((atoms, rows), BF))
    )(sends, node, cot)
    recv = lax.all_to_all(send_rows, "atoms", split_axis=0, concat_axis=0, tiled=True)
    cots = lax.all_gather(cot_rows, "chan", axis=0, tiled=False)
    valid = (
        jnp.arange(halo, dtype=jnp.int32)[None, :] < halo_count[:, 0][:, None]
    ).astype(F32).reshape(slots, 1)
    g_shapes = (
        sds((7 * channels, edges), BF),
        sds((6 * channels, 2 * edges), BF),
        sds((5 * channels, 2 * edges), BF),
    )
    d_shapes = (
        sds((7 * channels, lz), F32),
        sds((6 * channels, l1), F32),
        sds((5 * channels, l2), F32),
    )
    made = call(
        frame_kernel,
        g_shapes + d_shapes,
        (
            pltpu.VMEM((235, edges), F32),
            pltpu.VMEM((rows, edges), F32),
            pltpu.VMEM((1, edges), F32),
            pltpu.VMEM((lz, edges), BF),
            pltpu.VMEM((l1, 2 * edges), BF),
            pltpu.VMEM((l2, 2 * edges), BF),
        ),
        flops=10**10,
    )(
        node,
        recv,
        cots,
        rotation,
        envelope.reshape(1, edges),
        src,
        tgt,
        edge_count.reshape(1, 1),
        valid,
    )
    gz, g1, g2 = made[:3]
    own, halo_rows = call(
        back_kernel,
        (sds((rows, atoms), F32), sds((slots, rows), BF)),
        (
            pltpu.VMEM((235, edges), F32),
            pltpu.VMEM((29 * width, edges), F32),
            pltpu.VMEM((rows, edges), BF),
        ),
        flops=10**10,
    )(
        gz,
        g1,
        g2,
        weight_zero.reshape(7 * width, 7 * channels),
        weight_one.reshape(12 * width, 6 * channels),
        weight_two.reshape(10 * width, 5 * channels),
        rotation,
        src,
    )
    back = lax.all_to_all(halo_rows, "atoms", split_axis=0, concat_axis=0, tiled=True)
    grad_x = call(join_kernel, sds((rows, atoms), F32))(own, back, sends)

    dz = made[3][:, : 7 * width].reshape(7, channels, 7, width)
    d1 = made[4].reshape(6, channels, 2, 6, width)
    d2 = made[5][:, : 10 * width].reshape(5, channels, 2, 5, width)
    dz = lax.psum_scatter(dz, "atoms", scatter_dimension=1, tiled=True)
    d1 = lax.psum_scatter(d1, "atoms", scatter_dimension=1, tiled=True)
    d2 = lax.psum_scatter(d2, "atoms", scatter_dimension=1, tiled=True)
    return (
        grad_x.reshape(49, width, atoms),
        dz.transpose(2, 3, 0, 1) * factor,
        d1.transpose(2, 3, 4, 0, 1) * factor,
        d2.transpose(2, 3, 4, 0, 1) * factor,
    )


def solution(mesh):
    in_specs = (
        P(None, "chan", "atoms"),
        P(None, "chan", "atoms"),
        P(None, "atoms"),
        P("atoms"),
        P("atoms"),
        P("atoms"),
        P("atoms"),
        P("atoms", None, None),
        P(None, "atoms"),
        P(None, "chan", None, None),
        P(None, None, "chan", None, None),
        P(None, None, "chan", None, None),
    )
    out_specs = (
        P(None, "chan", "atoms"),
        P(None, "chan", None, "atoms"),
        P(None, None, "chan", None, "atoms"),
        P(None, None, "chan", None, "atoms"),
    )
    return jax.shard_map(
        on_device, mesh=mesh, in_specs=in_specs, out_specs=out_specs, check_vma=False
    )
```

```python
import functools
import math

import jax
import jax.numpy as jnp
from jax import lax
from jax.experimental import pallas as pl
from jax.experimental.pallas import tpu as pltpu
from jax.sharding import PartitionSpec as P

LANES = 128
BF = jnp.bfloat16
F32 = jnp.float32
VMEM_LIMIT = 56 * 1024 * 1024
MESH = pl.DeviceIdType.MESH


def dot(a, b, dims):
    return lax.dot_general(a, b, (dims, ((), ())), preferred_element_type=F32)


NN = ((1,), (0,))
NT = ((1,), (1,))
TN = ((0,), (0,))


def degrees(low=0, high=7):
    offset = 0
    for degree in range(high):
        reach = min(degree, 2)
        if degree >= low:
            yield degree, reach, offset
        offset += (2 * reach + 1) * (2 * degree + 1)


def cols(block, base=0):
    return pl.ds(pl.multiple_of(base + block * LANES, LANES), LANES)


def rotate_in(rot, raw, block, width, put, low=0, high=7):
    e = cols(block)
    for degree, reach, offset in degrees(low, high):
        breadth = 2 * degree + 1
        acc = [None] * (2 * reach + 1)
        for k in range(breadth):
            v = raw[pl.ds((degree * degree + k) * width, width), e]
            for r in range(2 * reach + 1):
                term = rot[pl.ds(offset + r * breadth + k, 1), e] * v
                acc[r] = term if acc[r] is None else acc[r] + term
        for r in range(2 * reach + 1):
            put(degree, r - reach, acc[r])


def rotate_out(rot, framed, block, width, out, low=0, high=7):
    e = cols(block)
    spots = {}
    for i, pair in enumerate(frame_pairs()):
        spots[pair] = i
    for degree, reach, offset in degrees(low, high):
        breadth = 2 * degree + 1
        u = [
            framed[pl.ds(spots[degree, m] * width, width), e]
            for m in range(-reach, reach + 1)
        ]
        for k in range(breadth):
            acc = None
            for r in range(2 * reach + 1):
                term = rot[pl.ds(offset + r * breadth + k, 1), e] * u[r]
                acc = term if acc is None else acc + term
            out[pl.ds((degree * degree + k) * width, width), e] = acc.astype(BF)


def frame_pairs():
    listing = [(degree, 0) for degree in range(7)]
    for order in (1, 2):
        listing = listing + [(degree, order) for degree in range(order, 7)]
        listing = listing + [(degree, -order) for degree in range(order, 7)]
    return listing


def onehot(ids, rows):
    return (lax.broadcasted_iota(jnp.int32, (rows, ids.shape[1]), 0) == ids).astype(BF)


def onehot_cols(ids, columns):
    return (lax.broadcasted_iota(jnp.int32, (ids.shape[0], columns), 1) == ids).astype(BF)


def prep_kernel(sends, node, cot, send_out, cot_out):
    atoms = node.shape[1]
    send_out[...] = dot(onehot_cols(sends[...], atoms), node[...], NT).astype(BF)
    eye = onehot_cols(lax.broadcasted_iota(jnp.int32, (atoms, 1), 0), atoms)
    cot_out[...] = dot(eye, cot[...], NT).astype(BF)


def frame_kernel(
    node,
    recv,
    cot,
    rotation,
    envelope,
    source,
    target,
    count,
    valid,
    gz,
    g1,
    g2,
    dz_out,
    d1_out,
    d2_out,
    rot,
    raw,
    radial,
    hz,
    h1,
    h2,
):
    atoms = node.shape[1]
    slots = recv.shape[0]
    edges = rotation.shape[1]
    blocks = edges // LANES
    groups = cot.shape[0]
    width = node.shape[0] // 49
    channels = gz.shape[0] // 7
    g12 = {1: g1, 2: g2}
    h12 = {1: h1, 2: h2}

    rot[...] = rotation[...].astype(F32)
    ids = source[...]
    own = onehot(ids, atoms)
    halo = onehot(ids - atoms, slots)
    usable = jnp.sum(halo.astype(F32) * valid[...], axis=0, keepdims=True)
    usable = jnp.where(ids < atoms, 1.0, usable)
    place = lax.broadcasted_iota(jnp.int32, (1, edges), 1)
    radial[...] = jnp.where(place < count[...], envelope[...] * usable, 0.0)
    to = onehot(target[...], atoms)

    def group(q, carry):
        raw[...] = dot(cot[q], to, TN)

        def one(block, carry):
            e = cols(block)
            scale = radial[:, e]

            def put(degree, m, value):
                value = (value * scale).astype(BF)
                order = abs(m)
                row = pl.ds(
                    pl.multiple_of((degree - order) * channels + q * width, width), width
                )
                if order == 0:
                    gz[row, e] = value
                else:
                    g12[order][row, cols(block, 0 if m > 0 else edges)] = value

            rotate_in(rot, raw, block, width, put)
            return carry

        return lax.fori_loop(0, blocks, one, carry)

    lax.fori_loop(0, groups, group, 0)

    raw[...] = dot(node[...], own, NN) + dot(recv[...], halo, TN)
    hz[...] = jnp.zeros_like(hz)
    h2[...] = jnp.zeros_like(h2)

    def one_h(block, carry):
        e = cols(block)
        later = cols(block, edges)

        def put(degree, m, value):
            value = value.astype(BF)
            order = abs(m)
            first = (degree - order) * width
            second = (7 - order + degree - order) * width
            if order == 0:
                hz[pl.ds(first, width), e] = value
            elif m > 0:
                h12[order][pl.ds(first, width), e] = value
                h12[order][pl.ds(second, width), later] = value
            else:
                h12[order][pl.ds(first, width), later] = value
                h12[order][pl.ds(second, width), e] = -value

        rotate_in(rot, raw, block, width, put)
        return carry

    lax.fori_loop(0, blocks, one_h, 0)

    dz_out[...] = dot(gz[...], hz[...], NT)
    d1_out[...] = dot(g1[...], h1[...], NT)
    d2_out[...] = dot(g2[...], h2[...], NT)


def back_kernel(gz, g1, g2, wz, w1, w2, rotation, source, own_out, halo_out, rot, fb, y):
    edges = rotation.shape[1]
    blocks = edges // LANES
    atoms = own_out.shape[1]
    slots = halo_out.shape[0]
    width = wz.shape[0] // 7
    rot[...] = rotation[...].astype(F32)
    fb[pl.ds(0, 7 * width), :] = dot(wz[...], gz[...], NN)
    start = 7 * width
    for count_l, w, g in ((6, w1, g1), (5, w2, g2)):
        rows = count_l * width
        real = dot(w[pl.ds(0, rows), :], g[...], NN)
        imag = dot(w[pl.ds(rows, rows), :], g[...], NN)
        fb[pl.ds(start, rows), :] = real[:, :edges] + imag[:, edges:]
        fb[pl.ds(start + rows, rows), :] = real[:, edges:] - imag[:, :edges]
        start += 2 * rows

    def one(block, carry):
        rotate_out(rot, fb, block, width, y)
        return carry

    lax.fori_loop(0, blocks, one, 0)
    ids = source[...]
    own_out[...] = dot(y[...], onehot(ids, atoms), NT)
    halo_out[...] = dot(onehot(ids - atoms, slots), y[...], NT).astype(BF)


def join_kernel(own, back, sends, out):
    out[...] = own[...] + dot(back[...], onehot_cols(sends[...], own.shape[1]), TN)


def column(row):
    n = row.shape[1]
    diag = lax.broadcasted_iota(jnp.int32, (n, n), 0) == lax.broadcasted_iota(
        jnp.int32, (n, n), 1
    )
    spread = jnp.where(diag, jnp.broadcast_to(row.astype(F32), (n, n)), 0.0)
    return jnp.sum(spread, axis=1, keepdims=True)


def whole_kernel(
    factor,
    sends_in,
    node_in,
    cot_in,
    rotation_in,
    envelope,
    source,
    target,
    count,
    counts_in,
    wz_in,
    w1_in,
    w2_in,
    x_out,
    total,
    node,
    cot,
    rotation,
    mine_a,
    mine_b,
    land_a,
    land_b,
    cots,
    rot,
    raw,
    radial,
    gz,
    g1,
    g2,
    hz,
    h1,
    h2,
    wz,
    w1,
    w2,
    fb,
    y,
    back_a,
    back_b,
    home_a,
    home_b,
    pieces,
    near,
    passing,
    relay,
    fin,
    halo_sent,
    halo_got,
    chan_sent,
    chan_got,
    near_sent,
    near_got,
    far_sent,
    relay_got,
    fin_got,
    back_sent,
    back_got,
    load_got,
    weight_got,
):
    parts, halo, cut = land_a.shape
    rows_x = node.shape[0]
    halves = ((0, 5, pl.ds(0, cut)), (5, 7, pl.ds(cut, rows_x - cut)))
    groups = cots.shape[0]
    atoms = node.shape[1]
    slots = parts * halo
    edges = rotation.shape[1]
    blocks = edges // LANES
    width = rows_x // 49
    channels = width * groups
    share = channels // parts
    me = lax.axis_index("atoms")
    group = lax.axis_index("chan")
    line, side = me // 2, lax.rem(me, 2)
    other = line * 2 + 1 - side
    mate = line + 1 - 2 * lax.rem(line, 2)
    inner = (line + 1) // 2 == 1
    across, core = group // 2, lax.rem(group, 2)

    def flipped(code):
        a = 1 - across if code >= 2 else across
        c = 1 - core if code % 2 else core
        return a * 2 + c

    far_pair = 1 - line // 2
    distant = (far_pair + across) % 2
    first_far, second_far = far_pair * 2 + core, far_pair * 2 + 1 - core
    steps = [
        mate * distant + first_far * (1 - distant),
        first_far * distant + second_far * (1 - distant),
        second_far * distant + mate * (1 - distant),
        line,
    ]

    place_in_pair = lax.rem(line, 2)
    partners = []
    for pair, spot, turn in (
        (1, 0, 0),
        (1, 1, 0),
        (1, 0, 1),
        (1, 1, 1),
        (0, 1, 0),
        (0, 1, 1),
        (0, 0, 1),
    ):
        there = (far_pair if pair else line // 2) * 2
        there = there + (1 - place_in_pair if spot else place_in_pair)
        partners.append(there * 2 + (1 - side if turn else side))

    def push(src, dst, sent, got, where):
        return pltpu.make_async_remote_copy(
            src_ref=src,
            dst_ref=dst,
            send_sem=sent,
            recv_sem=got,
            device_id=where,
            device_id_type=MESH,
        )

    loads = []
    for slot, (src, dst) in enumerate(((node_in, node), (cot_in, cot), (rotation_in, rotation))):
        copy = pltpu.make_async_copy(src, dst, load_got.at[slot])
        copy.start()
        loads.append(copy)
    barrier = pltpu.get_barrier_semaphore()
    for k in range(1, parts):
        pl.semaphore_signal(
            barrier, inc=1, device_id={"atoms": lax.rem(me + k, parts)}, device_id_type=MESH
        )
    for code in (1, 2):
        pl.semaphore_signal(
            barrier, inc=1, device_id={"chan": flipped(code)}, device_id_type=MESH
        )
    sends = jnp.concatenate([column(sends_in[p : p + 1, :]) for p in range(parts)], axis=0)
    sends = sends.astype(jnp.int32)
    loads[0].wait()
    pick = onehot_cols(sends, atoms)
    for mine, (low, high, span) in zip((mine_a, mine_b), halves):
        picked = dot(pick, node[span, :], NT).astype(BF)
        for p in range(parts):
            mine[p] = picked[p * halo : (p + 1) * halo, :]
    pl.semaphore_wait(barrier, parts + 1)

    halo_copies = []
    for part, (mine, land) in enumerate(((mine_a, land_a), (mine_b, land_b))):
        for k, peer in enumerate(partners):
            copy = push(
                mine.at[peer],
                land.at[me],
                halo_sent.at[part, k],
                halo_got.at[part, k],
                {"atoms": peer},
            )
            copy.start()
            halo_copies.append(copy)
    eye = onehot_cols(lax.broadcasted_iota(jnp.int32, (atoms, 1), 0), atoms)
    loads[1].wait()
    cots[group] = dot(eye, cot[...], NT).astype(BF)

    def chan_copy(slot, which, code):
        return push(
            cots.at[which],
            cots.at[which],
            chan_sent.at[slot],
            chan_got.at[slot],
            {"chan": flipped(code)},
        )

    chan_copies = [chan_copy(0, group, 1), chan_copy(1, group, 2)]
    for copy in chan_copies:
        copy.start()
    land_a[me] = mine_a[me]
    land_b[me] = mine_b[me]
    weight_loads = []
    for src, dst in ((wz_in, wz), (w1_in, w1), (w2_in, w2)):
        lead = (slice(None),) * (len(src.shape) - 4)
        for j in range(src.shape[-3]):
            copy = pltpu.make_async_copy(
                src.at[lead + (slice(None), j)],
                dst.at[lead + (slice(None), slice(None), pl.ds(j * channels, channels))],
                weight_got.at[len(weight_loads)],
            )
            copy.start()
            weight_loads.append(copy)

    loads[2].wait()
    rot[...] = rotation[...].astype(F32)
    ids = source[...]
    own = onehot(ids, atoms)
    remote = onehot(ids - atoms, slots)
    order = lax.broadcasted_iota(jnp.int32, (halo, 1), 0)
    valid = jnp.concatenate(
        [(order < counts_in[:, p : p + 1]).astype(F32) for p in range(parts)], axis=0
    )
    usable = jnp.sum(remote.astype(F32) * valid, axis=0, keepdims=True)
    usable = jnp.where(ids < atoms, 1.0, usable)
    place = lax.broadcasted_iota(jnp.int32, (1, edges), 1)
    radial[...] = jnp.where(place < count[...], envelope[...] * usable, 0.0)
    to = onehot(target[...], atoms)

    g12 = {1: g1, 2: g2}
    h12 = {1: h1, 2: h2}

    def frame_grad(q, low=0, high=blocks):
        if low == 0:
            raw[...] = dot(cots[q], to, TN)

        def one(block, carry):
            e = cols(block)
            scale = radial[:, e]

            def put(degree, m, value):
                value = (value * scale).astype(BF)
                o = abs(m)
                row = pl.ds(
                    pl.multiple_of((degree - o) * channels + q * width, width), width
                )
                if o == 0:
                    gz[row, e] = value
                else:
                    g12[o][row, cols(block, 0 if m > 0 else edges)] = value

            rotate_in(rot, raw, block, width, put)
            return carry

        lax.fori_loop(low, high, one, 0)

    def one_h(low, high, block, carry):
        e = cols(block)
        later = cols(block, edges)

        def put(degree, m, value):
            value = value.astype(BF)
            o = abs(m)
            first = (degree - o) * width
            spot = 7 - o + degree - o
            if o == 2 and spot >= 8:
                spot = 11 if spot == 8 else 8
            second = spot * width
            if o == 0:
                hz[pl.ds(first, width), e] = value
            elif m > 0:
                h12[o][pl.ds(first, width), e] = value
                h12[o][pl.ds(second, width), later] = value
            else:
                h12[o][pl.ds(first, width), later] = value
                h12[o][pl.ds(second, width), e] = -value

        rotate_in(rot, raw, block, width, put, low, high)
        return carry

    spans = []
    base = 0
    for rows in (14 * share, 18 * share, 11 * share):
        spans.append(pl.ds(base, rows))
        base += rows
    near_copies = {}
    lane = lax.broadcasted_iota(jnp.int32, (1, LANES), 1)

    def weight_piece(k):
        q = steps[k]

        def left(g, count_l):
            return jnp.concatenate(
                [
                    g[pl.ds(pl.multiple_of(l * channels + q * width, width), width), :]
                    for l in range(count_l)
                ],
                axis=0,
            )

        def place(start, value):
            value = value.astype(BF)
            for degree in range(value.shape[0] // width):
                for half in range(2):
                    row = degree * width + half * share
                    at = start + degree * share
                    pieces[k, half, at : at + share, :] = value[row : row + share, :]

        left_two = left(g2, 5)
        tail = dot(left_two, h2[pl.ds(2 * LANES, LANES), :], NT)
        part = dot(left(gz, 7), hz[...], NT)
        last = jnp.concatenate([tail, pltpu.roll(tail[: 2 * width], 3 * width, 1)], axis=0)
        place(0, part[:, :LANES])
        place(7 * share, jnp.where(lane < 3 * width, part[:, LANES:], last))
        send_near(k, 0)
        part = dot(left(g1, 6), h1[...], NT)
        for tile in range(3):
            place(spans[1].start + tile * 6 * share, part[:, tile * LANES : (tile + 1) * LANES])
        send_near(k, 1)
        part = dot(left_two, h2[pl.ds(0, 2 * LANES), :], NT)
        for tile in range(2):
            place(spans[2].start + tile * 5 * share, part[:, tile * LANES : (tile + 1) * LANES])
        third = pltpu.roll(tail[3 * width : 4 * width], width, 1)
        fourth = pltpu.roll(tail[4 * width :], 2 * width, 1)
        third = jnp.where(lane < 2 * width, third, fourth)
        place(spans[2].start + 10 * share, jnp.where(lane < width, tail[2 * width : 3 * width], third))
        send_near(k, 2)

    def send_near(k, c):
        copy = push(
            pieces.at[k, 1 - side, spans[c]],
            near.at[k, spans[c]],
            near_sent.at[k, c],
            near_got.at[k, c],
            {"atoms": other},
        )
        copy.start()
        near_copies[k, c] = copy

    def relay_copy(k, c):
        return push(
            passing.at[k, spans[c]],
            relay.at[k, spans[c]],
            far_sent.at[k, c],
            relay_got.at[k, c],
            {"atoms": mate * 2 + side},
        )

    def fin_copy(k, c, slot, q):
        return push(
            passing.at[k, spans[c]],
            fin.at[slot, spans[c]],
            far_sent.at[k, c],
            fin_got.at[slot, c],
            {"atoms": q * 2 + side},
        )

    def summed(k, c):
        return pieces[k, side, spans[c]].astype(F32) + near[k, spans[c]].astype(F32)

    def pass_on(k, c):
        near_copies[k, c].wait_recv()
        if k == groups - 1:
            total[spans[c], :] = summed(k, c)
            return

        @pl.when(steps[k] == mate)
        def direct():
            passing[k, spans[c], :] = summed(k, c).astype(BF)
            fin_copy(k, c, 0, mate).start()

        @pl.when((steps[k] != mate) & jnp.logical_not(inner))
        def hand():
            passing[k, spans[c], :] = summed(k, c).astype(BF)
            relay_copy(k, c).start()

    def relay_on(k, c):
        @pl.when((steps[k] != mate) & inner)
        def join():
            relay_copy(k, c).wait_recv()
            value = summed(k, c) + relay[k, spans[c]].astype(F32)
            passing[k, spans[c], :] = value.astype(BF)
            fin_copy(k, c, 1, steps[k]).start()

    frame_grad(group)
    chan_copies[0].wait_recv()
    frame_grad(flipped(1))
    hz[...] = jnp.zeros_like(hz)
    h2[...] = jnp.zeros_like(h2)

    def whole(land):
        return land[...].astype(F32).reshape(slots, land.shape[2]).astype(BF)

    for part, (land, (low, high, span)) in enumerate(zip((land_a, land_b), halves)):
        for copy in halo_copies[part * (parts - 1) : (part + 1) * (parts - 1)]:
            copy.wait_recv()
        raw[span, :] = dot(node[span, :], own, NN) + dot(whole(land), remote, TN)
        lax.fori_loop(0, blocks, functools.partial(one_h, low, high), 0)
    weight_piece(0)

    chan_copies[1].wait_recv()
    chan_copies.append(chan_copy(2, flipped(2), 1))
    chan_copies[2].start()
    frame_grad(flipped(2))
    weight_piece(1)
    pass_on(0, 0)
    chan_copies[2].wait_recv()
    frame_grad(flipped(3), 0, blocks // 2)
    pass_on(0, 1)
    frame_grad(flipped(3), blocks // 2, blocks)
    pass_on(0, 2)
    weight_piece(2)

    for copy in weight_loads:
        copy.wait()
    fb[pl.ds(0, 7 * width), :] = dot(wz[...].reshape(7 * width, 7 * channels), gz[...], NN)
    pass_on(1, 0)
    start = 7 * width
    for count_l, w, g in ((6, w1, g1), (5, w2, g2)):
        rows = count_l * width
        real = dot(w[0].reshape(rows, count_l * channels), g[...], NN)
        imag = dot(w[1].reshape(rows, count_l * channels), g[...], NN)
        fb[pl.ds(start, rows), :] = real[:, :edges] + imag[:, edges:]
        fb[pl.ds(start + rows, rows), :] = real[:, edges:] - imag[:, :edges]
        start += 2 * rows
    pass_on(1, 1)
    for c in range(2):
        relay_on(0, c)

    def one_back(low, high, block, carry):
        rotate_out(rot, fb, block, width, y, low, high)
        return carry

    back_copies = []
    for part, (back, home, (low, high, span)) in enumerate(
        zip((back_a, back_b), (home_a, home_b), halves)
    ):
        lax.fori_loop(0, blocks, functools.partial(one_back, low, high), 0)
        terms = dot(remote, y[span, :], NT).astype(BF)
        for p in range(parts):
            back[p] = terms[p * halo : (p + 1) * halo, :]
        for k in range(1, parts):
            peer = lax.rem(me + k, parts)
            copy = push(
                back.at[peer],
                home.at[me],
                back_sent.at[part, k],
                back_got.at[part, k],
                {"atoms": peer},
            )
            copy.start()
            back_copies.append(copy)
    pass_on(1, 2)
    relay_on(0, 2)
    pass_on(2, 0)
    pass_on(2, 1)
    weight_piece(3)
    relay_on(1, 0)
    relay_on(1, 1)
    pass_on(2, 2)
    relay_on(1, 2)
    x_out[...] = dot(y[...], own, NT)
    home_a[me] = back_a[me]
    home_b[me] = back_b[me]
    relay_on(2, 0)
    relay_on(2, 1)
    relay_on(2, 2)
    pass_on(3, 0)
    pass_on(3, 1)
    pass_on(3, 2)
    for part, (home, (low, high, span)) in enumerate(zip((home_a, home_b), halves)):
        for copy in back_copies[part * (parts - 1) : (part + 1) * (parts - 1)]:
            copy.wait_recv()
        x_out[span, :] += dot(whole(home), pick, TN)

    for c in range(3):
        value = total[spans[c], :]
        for slot in range(2):
            fin_copy(0, c, slot, mate).wait_recv()
            value = value + fin[slot, spans[c]].astype(F32)
        total[spans[c], :] = value * factor

    for copy in halo_copies + chan_copies + list(near_copies.values()) + back_copies:
        copy.wait_send()
    for k in range(groups - 1):
        for c in range(3):
            relay_copy(k, c).wait_send()


def write_kernel(x, total, x_out, dz_out, d1_out, d2_out):
    x_out[...] = x[...]
    share, width = dz_out.shape[-2:]

    def cut(slot, spot):
        return total[slot * share : (slot + 1) * share, spot * width : (spot + 1) * width]

    for i in range(7):
        tile, spot = divmod(i, 4)
        for j in range(7):
            dz_out[i, j] = cut(tile * 7 + j, spot)
    for i in range(12):
        tile, spot = divmod(i, 4)
        for j in range(6):
            d1_out[i // 6, i % 6, j] = cut(14 + tile * 6 + j, spot)
    for i in range(10):
        tile, spot = divmod(i, 4)
        for j in range(5):
            if i < 8:
                where = (32 + tile * 5 + j, spot)
            elif i == 8:
                where = (7 + j, 3)
            else:
                where = (12 + j, 3) if j < 2 else (42, j - 2)
            d2_out[i // 5, i % 5, j] = cut(*where)


def call(kernel, outs, scratch=(), flops=10**8, collective=None, specs=None):
    if collective is None:
        params = pltpu.CompilerParams(vmem_limit_bytes=VMEM_LIMIT)
    else:
        params = pltpu.CompilerParams(
            vmem_limit_bytes=VMEM_LIMIT, collective_id=collective, has_side_effects=True
        )
    extra = {} if specs is None else {"in_specs": specs}
    return pl.pallas_call(
        kernel,
        out_shape=outs,
        **extra,
        scratch_shapes=list(scratch),
        compiler_params=params,
        cost_estimate=pl.CostEstimate(
            flops=flops, bytes_accessed=8 * 10**6, transcendentals=0
        ),
    )


def on_device(
    node_x,
    cotangent,
    rotation,
    envelope,
    source,
    target,
    edge_count,
    send_index,
    halo_count,
    weight_zero,
    weight_one,
    weight_two,
):
    parts = lax.axis_size("atoms")
    groups = lax.axis_size("chan")
    width = node_x.shape[1]
    channels = width * groups
    atoms = node_x.shape[2]
    halo = send_index.shape[2]
    edges = source.shape[0]
    slots = parts * halo
    rows = 49 * width
    share = channels // parts
    fast = parts == 8 and groups == 4 and share % 16 == 0 and width == 2 * share
    sds = jax.ShapeDtypeStruct

    node = node_x.reshape(rows, atoms)
    cot = cotangent.reshape(rows, atoms)
    factor = 1.0 / math.sqrt(edges * parts)
    src = source.reshape(1, edges)
    tgt = target.reshape(1, edges)
    pad = lambda n: -(-n // LANES) * LANES
    lz, l1, l2 = pad(7 * width), pad(12 * width), pad(10 * width)

    if fast:
        height = 43 * share
        vmem = pltpu.VMEM
        dma = pltpu.SemaphoreType.DMA
        grad_x, summed = call(
            functools.partial(whole_kernel, factor),
            (sds((rows, atoms), F32), sds((height, LANES), F32)),
            (
                vmem((rows, atoms), BF),
                vmem((rows, atoms), BF),
                vmem((235, edges), BF),
                vmem((parts, halo, 25 * width), BF),
                vmem((parts, halo, 24 * width), BF),
                vmem((parts, halo, 25 * width), BF),
                vmem((parts, halo, 24 * width), BF),
                vmem((groups, atoms, rows), BF),
                vmem((235, edges), F32),
                vmem((rows, edges), F32),
                vmem((1, edges), F32),
                vmem((7 * channels, edges), BF),
                vmem((6 * channels, 2 * edges), BF),
                vmem((5 * channels, 2 * edges), BF),
                vmem((lz, edges), BF),
                vmem((l1, 2 * edges), BF),
                vmem((l2, 2 * edges), BF),
                vmem((7, width, 7 * channels), BF),
                vmem((2, 6, width, 6 * channels), BF),
                vmem((2, 5, width, 5 * channels), BF),
                vmem((29 * width, edges), F32),
                vmem((rows, edges), BF),
                vmem((parts, halo, 25 * width), BF),
                vmem((parts, halo, 24 * width), BF),
                vmem((parts, halo, 25 * width), BF),
                vmem((parts, halo, 24 * width), BF),
                vmem((groups, 2, height, LANES), BF),
                vmem((groups, height, LANES), BF),
                vmem((groups, height, LANES), BF),
                vmem((groups, height, LANES), BF),
                vmem((2, height, LANES), BF),
                dma((2, parts)),
                dma((2, parts)),
                dma((3,)),
                dma((3,)),
                dma((groups, 3)),
                dma((groups, 3)),
                dma((groups, 3)),
                dma((groups, 3)),
                dma((2, 3)),
                dma((2, parts)),
                dma((2, parts)),
                dma((3,)),
                dma((18,)),
            ),
            flops=10**10,
            collective=0,
            specs=[
                pl.BlockSpec(memory_space=pltpu.HBM if far else pltpu.VMEM)
                for far in (0, 1, 1, 1, 0, 0, 0, 0, 0, 1, 1, 1)
            ],
        )(
            send_index[0],
            node,
            cot,
            rotation,
            envelope.reshape(1, edges),
            src,
            tgt,
            edge_count.reshape(1, 1),
            halo_count.reshape(1, parts),
            weight_zero.transpose(0, 2, 1, 3),
            weight_one.transpose(0, 1, 3, 2, 4),
            weight_two.transpose(0, 1, 3, 2, 4),
        )
        grad_x, dz, d1, d2 = call(
            write_kernel,
            (
                sds((rows, atoms), F32),
                sds((7, 7, share, width), F32),
                sds((2, 6, 6, share, width), F32),
                sds((2, 5, 5, share, width), F32),
            ),
        )(grad_x, summed)
        return (
            grad_x.reshape(49, width, atoms),
            dz.transpose(0, 3, 1, 2),
            d1.transpose(0, 1, 4, 2, 3),
            d2.transpose(0, 1, 4, 2, 3),
        )

    sends = send_index.reshape(slots, 1)
    send_rows, cot_rows = call(
        prep_kernel, (sds((slots, rows), BF), sds((atoms, rows), BF))
    )(sends, node, cot)
    recv = lax.all_to_all(send_rows, "atoms", split_axis=0, concat_axis=0, tiled=True)
    cots = lax.all_gather(cot_rows, "chan", axis=0, tiled=False)
    valid = (
        jnp.arange(halo, dtype=jnp.int32)[None, :] < halo_count[:, 0][:, None]
    ).astype(F32).reshape(slots, 1)
    g_shapes = (
        sds((7 * channels, edges), BF),
        sds((6 * channels, 2 * edges), BF),
        sds((5 * channels, 2 * edges), BF),
    )
    d_shapes = (
        sds((7 * channels, lz), F32),
        sds((6 * channels, l1), F32),
        sds((5 * channels, l2), F32),
    )
    made = call(
        frame_kernel,
        g_shapes + d_shapes,
        (
            pltpu.VMEM((235, edges), F32),
            pltpu.VMEM((rows, edges), F32),
            pltpu.VMEM((1, edges), F32),
            pltpu.VMEM((lz, edges), BF),
            pltpu.VMEM((l1, 2 * edges), BF),
            pltpu.VMEM((l2, 2 * edges), BF),
        ),
        flops=10**10,
    )(
        node,
        recv,
        cots,
        rotation,
        envelope.reshape(1, edges),
        src,
        tgt,
        edge_count.reshape(1, 1),
        valid,
    )
    gz, g1, g2 = made[:3]
    own, halo_rows = call(
        back_kernel,
        (sds((rows, atoms), F32), sds((slots, rows), BF)),
        (
            pltpu.VMEM((235, edges), F32),
            pltpu.VMEM((29 * width, edges), F32),
            pltpu.VMEM((rows, edges), BF),
        ),
        flops=10**10,
    )(
        gz,
        g1,
        g2,
        weight_zero.reshape(7 * width, 7 * channels),
        weight_one.reshape(12 * width, 6 * channels),
        weight_two.reshape(10 * width, 5 * channels),
        rotation,
        src,
    )
    back = lax.all_to_all(halo_rows, "atoms", split_axis=0, concat_axis=0, tiled=True)
    grad_x = call(join_kernel, sds((rows, atoms), F32))(own, back, sends)

    dz = made[3][:, : 7 * width].reshape(7, channels, 7, width)
    d1 = made[4].reshape(6, channels, 2, 6, width)
    d2 = made[5][:, : 10 * width].reshape(5, channels, 2, 5, width)
    dz = lax.psum_scatter(dz, "atoms", scatter_dimension=1, tiled=True)
    d1 = lax.psum_scatter(d1, "atoms", scatter_dimension=1, tiled=True)
    d2 = lax.psum_scatter(d2, "atoms", scatter_dimension=1, tiled=True)
    return (
        grad_x.reshape(49, width, atoms),
        dz.transpose(2, 3, 0, 1) * factor,
        d1.transpose(2, 3, 4, 0, 1) * factor,
        d2.transpose(2, 3, 4, 0, 1) * factor,
    )


def solution(mesh):
    in_specs = (
        P(None, "chan", "atoms"),
        P(None, "chan", "atoms"),
        P(None, "atoms"),
        P("atoms"),
        P("atoms"),
        P("atoms"),
        P("atoms"),
        P("atoms", None, None),
        P(None, "atoms"),
        P(None, "chan", None, None),
        P(None, None, "chan", None, None),
        P(None, None, "chan", None, None),
    )
    out_specs = (
        P(None, "chan", "atoms"),
        P(None, "chan", None, "atoms"),
        P(None, None, "chan", None, "atoms"),
        P(None, None, "chan", None, "atoms"),
    )
    return jax.shard_map(
        on_device, mesh=mesh, in_specs=in_specs, out_specs=out_specs, check_vma=False
    )
```

```python
import functools
import math

import jax
import jax.numpy as jnp
from jax import lax
from jax.experimental import pallas as pl
from jax.experimental.pallas import tpu as pltpu
from jax.sharding import PartitionSpec as P

LANES = 128
BF = jnp.bfloat16
F32 = jnp.float32
VMEM_LIMIT = 56 * 1024 * 1024
MESH = pl.DeviceIdType.MESH


def dot(a, b, dims):
    return lax.dot_general(a, b, (dims, ((), ())), preferred_element_type=F32)


NN = ((1,), (0,))
NT = ((1,), (1,))
TN = ((0,), (0,))


def degrees(low=0, high=7):
    offset = 0
    for degree in range(high):
        reach = min(degree, 2)
        if degree >= low:
            yield degree, reach, offset
        offset += (2 * reach + 1) * (2 * degree + 1)


def cols(block, base=0):
    return pl.ds(pl.multiple_of(base + block * LANES, LANES), LANES)


def rotate_in(rot, raw, block, width, put, low=0, high=7):
    e = cols(block)
    for degree, reach, offset in degrees(low, high):
        breadth = 2 * degree + 1
        acc = [None] * (2 * reach + 1)
        for k in range(breadth):
            v = raw[pl.ds((degree * degree + k) * width, width), e]
            for r in range(2 * reach + 1):
                term = rot[pl.ds(offset + r * breadth + k, 1), e] * v
                acc[r] = term if acc[r] is None else acc[r] + term
        for r in range(2 * reach + 1):
            put(degree, r - reach, acc[r])


def rotate_out(rot, framed, block, width, out, low=0, high=7):
    e = cols(block)
    spots = {}
    for i, pair in enumerate(frame_pairs()):
        spots[pair] = i
    for degree, reach, offset in degrees(low, high):
        breadth = 2 * degree + 1
        u = [
            framed[pl.ds(spots[degree, m] * width, width), e]
            for m in range(-reach, reach + 1)
        ]
        for k in range(breadth):
            acc = None
            for r in range(2 * reach + 1):
                term = rot[pl.ds(offset + r * breadth + k, 1), e] * u[r]
                acc = term if acc is None else acc + term
            out[pl.ds((degree * degree + k) * width, width), e] = acc.astype(BF)


def frame_pairs():
    listing = [(degree, 0) for degree in range(7)]
    for order in (1, 2):
        listing = listing + [(degree, order) for degree in range(order, 7)]
        listing = listing + [(degree, -order) for degree in range(order, 7)]
    return listing


def onehot(ids, rows):
    return (lax.broadcasted_iota(jnp.int32, (rows, ids.shape[1]), 0) == ids).astype(BF)


def onehot_cols(ids, columns):
    return (lax.broadcasted_iota(jnp.int32, (ids.shape[0], columns), 1) == ids).astype(BF)


def prep_kernel(sends, node, cot, send_out, cot_out):
    atoms = node.shape[1]
    send_out[...] = dot(onehot_cols(sends[...], atoms), node[...], NT).astype(BF)
    eye = onehot_cols(lax.broadcasted_iota(jnp.int32, (atoms, 1), 0), atoms)
    cot_out[...] = dot(eye, cot[...], NT).astype(BF)


def frame_kernel(
    node,
    recv,
    cot,
    rotation,
    envelope,
    source,
    target,
    count,
    valid,
    gz,
    g1,
    g2,
    dz_out,
    d1_out,
    d2_out,
    rot,
    raw,
    radial,
    hz,
    h1,
    h2,
):
    atoms = node.shape[1]
    slots = recv.shape[0]
    edges = rotation.shape[1]
    blocks = edges // LANES
    groups = cot.shape[0]
    width = node.shape[0] // 49
    channels = gz.shape[0] // 7
    g12 = {1: g1, 2: g2}
    h12 = {1: h1, 2: h2}

    rot[...] = rotation[...].astype(F32)
    ids = source[...]
    own = onehot(ids, atoms)
    halo = onehot(ids - atoms, slots)
    usable = jnp.sum(halo.astype(F32) * valid[...], axis=0, keepdims=True)
    usable = jnp.where(ids < atoms, 1.0, usable)
    place = lax.broadcasted_iota(jnp.int32, (1, edges), 1)
    radial[...] = jnp.where(place < count[...], envelope[...] * usable, 0.0)
    to = onehot(target[...], atoms)

    def group(q, carry):
        raw[...] = dot(cot[q], to, TN)

        def one(block, carry):
            e = cols(block)
            scale = radial[:, e]

            def put(degree, m, value):
                value = (value * scale).astype(BF)
                order = abs(m)
                row = pl.ds(
                    pl.multiple_of((degree - order) * channels + q * width, width), width
                )
                if order == 0:
                    gz[row, e] = value
                else:
                    g12[order][row, cols(block, 0 if m > 0 else edges)] = value

            rotate_in(rot, raw, block, width, put)
            return carry

        return lax.fori_loop(0, blocks, one, carry)

    lax.fori_loop(0, groups, group, 0)

    raw[...] = dot(node[...], own, NN) + dot(recv[...], halo, TN)
    hz[...] = jnp.zeros_like(hz)
    h2[...] = jnp.zeros_like(h2)

    def one_h(block, carry):
        e = cols(block)
        later = cols(block, edges)

        def put(degree, m, value):
            value = value.astype(BF)
            order = abs(m)
            first = (degree - order) * width
            second = (7 - order + degree - order) * width
            if order == 0:
                hz[pl.ds(first, width), e] = value
            elif m > 0:
                h12[order][pl.ds(first, width), e] = value
                h12[order][pl.ds(second, width), later] = value
            else:
                h12[order][pl.ds(first, width), later] = value
                h12[order][pl.ds(second, width), e] = -value

        rotate_in(rot, raw, block, width, put)
        return carry

    lax.fori_loop(0, blocks, one_h, 0)

    dz_out[...] = dot(gz[...], hz[...], NT)
    d1_out[...] = dot(g1[...], h1[...], NT)
    d2_out[...] = dot(g2[...], h2[...], NT)


def back_kernel(gz, g1, g2, wz, w1, w2, rotation, source, own_out, halo_out, rot, fb, y):
    edges = rotation.shape[1]
    blocks = edges // LANES
    atoms = own_out.shape[1]
    slots = halo_out.shape[0]
    width = wz.shape[0] // 7
    rot[...] = rotation[...].astype(F32)
    fb[pl.ds(0, 7 * width), :] = dot(wz[...], gz[...], NN)
    start = 7 * width
    for count_l, w, g in ((6, w1, g1), (5, w2, g2)):
        rows = count_l * width
        real = dot(w[pl.ds(0, rows), :], g[...], NN)
        imag = dot(w[pl.ds(rows, rows), :], g[...], NN)
        fb[pl.ds(start, rows), :] = real[:, :edges] + imag[:, edges:]
        fb[pl.ds(start + rows, rows), :] = real[:, edges:] - imag[:, :edges]
        start += 2 * rows

    def one(block, carry):
        rotate_out(rot, fb, block, width, y)
        return carry

    lax.fori_loop(0, blocks, one, 0)
    ids = source[...]
    own_out[...] = dot(y[...], onehot(ids, atoms), NT)
    halo_out[...] = dot(onehot(ids - atoms, slots), y[...], NT).astype(BF)


def join_kernel(own, back, sends, out):
    out[...] = own[...] + dot(back[...], onehot_cols(sends[...], own.shape[1]), TN)


def column(row):
    n = row.shape[1]
    diag = lax.broadcasted_iota(jnp.int32, (n, n), 0) == lax.broadcasted_iota(
        jnp.int32, (n, n), 1
    )
    spread = jnp.where(diag, jnp.broadcast_to(row.astype(F32), (n, n)), 0.0)
    return jnp.sum(spread, axis=1, keepdims=True)


def whole_kernel(
    factor,
    sends_in,
    node_in,
    cot_in,
    rotation_in,
    envelope,
    source,
    target,
    count,
    counts_in,
    wz_in,
    w1_in,
    w2_in,
    x_out,
    total,
    node,
    cot,
    rotation,
    mine_a,
    mine_b,
    land_a,
    land_b,
    cots,
    rot,
    raw,
    radial,
    gz,
    g1,
    g2,
    hz,
    h1,
    h2,
    wz,
    w1,
    w2,
    fb,
    y,
    back_a,
    back_b,
    home_a,
    home_b,
    pieces,
    near,
    passing,
    relay,
    fin,
    halo_sent,
    halo_got,
    chan_sent,
    chan_got,
    near_sent,
    near_got,
    far_sent,
    relay_got,
    fin_got,
    back_sent,
    back_got,
    load_got,
    weight_got,
):
    parts, halo, cut = land_a.shape
    rows_x = node.shape[0]
    halves = ((0, 5, pl.ds(0, cut)), (5, 7, pl.ds(cut, rows_x - cut)))
    groups = cots.shape[0]
    atoms = node.shape[1]
    slots = parts * halo
    edges = rotation.shape[1]
    blocks = edges // LANES
    width = rows_x // 49
    channels = width * groups
    share = channels // parts
    me = lax.axis_index("atoms")
    group = lax.axis_index("chan")
    line, side = me // 2, lax.rem(me, 2)
    other = line * 2 + 1 - side
    mate = line + 1 - 2 * lax.rem(line, 2)
    inner = (line + 1) // 2 == 1
    across, core = group // 2, lax.rem(group, 2)

    def flipped(code):
        a = 1 - across if code >= 2 else across
        c = 1 - core if code % 2 else core
        return a * 2 + c

    far_pair = 1 - line // 2
    distant = (far_pair + across) % 2
    first_far, second_far = far_pair * 2 + core, far_pair * 2 + 1 - core
    steps = [
        mate * distant + first_far * (1 - distant),
        first_far * distant + second_far * (1 - distant),
        second_far * distant + mate * (1 - distant),
        line,
    ]

    place_in_pair = lax.rem(line, 2)
    partners = []
    for pair, spot, turn in (
        (1, 0, 0),
        (1, 1, 0),
        (1, 0, 1),
        (1, 1, 1),
        (0, 1, 0),
        (0, 1, 1),
        (0, 0, 1),
    ):
        there = (far_pair if pair else line // 2) * 2
        there = there + (1 - place_in_pair if spot else place_in_pair)
        partners.append(there * 2 + (1 - side if turn else side))

    def push(src, dst, sent, got, where):
        return pltpu.make_async_remote_copy(
            src_ref=src,
            dst_ref=dst,
            send_sem=sent,
            recv_sem=got,
            device_id=where,
            device_id_type=MESH,
        )

    loads = []
    for slot, (src, dst) in enumerate(((node_in, node), (cot_in, cot), (rotation_in, rotation))):
        copy = pltpu.make_async_copy(src, dst, load_got.at[slot])
        copy.start()
        loads.append(copy)
    barrier = pltpu.get_barrier_semaphore()
    for k in range(1, parts):
        pl.semaphore_signal(
            barrier, inc=1, device_id={"atoms": lax.rem(me + k, parts)}, device_id_type=MESH
        )
    for code in (1, 2):
        pl.semaphore_signal(
            barrier, inc=1, device_id={"chan": flipped(code)}, device_id_type=MESH
        )
    sends = jnp.concatenate([column(sends_in[p : p + 1, :]) for p in range(parts)], axis=0)
    sends = sends.astype(jnp.int32)
    loads[0].wait()
    pick = onehot_cols(sends, atoms)
    for mine, (low, high, span) in zip((mine_a, mine_b), halves):
        picked = dot(pick, node[span, :], NT).astype(BF)
        for p in range(parts):
            mine[p] = picked[p * halo : (p + 1) * halo, :]
    eye = onehot_cols(lax.broadcasted_iota(jnp.int32, (atoms, 1), 0), atoms)
    loads[1].wait()
    cots[group] = dot(eye, cot[...], NT).astype(BF)
    pl.semaphore_wait(barrier, parts + 1)

    halo_copies = []
    for part, (mine, land) in enumerate(((mine_a, land_a), (mine_b, land_b))):
        for k, peer in enumerate(partners):
            copy = push(
                mine.at[peer],
                land.at[me],
                halo_sent.at[part, k],
                halo_got.at[part, k],
                {"atoms": peer},
            )
            copy.start()
            halo_copies.append(copy)

    def chan_copy(slot, which, code):
        return push(
            cots.at[which],
            cots.at[which],
            chan_sent.at[slot],
            chan_got.at[slot],
            {"chan": flipped(code)},
        )

    chan_copies = [chan_copy(0, group, 1), chan_copy(1, group, 2)]
    for copy in chan_copies:
        copy.start()
    land_a[me] = mine_a[me]
    land_b[me] = mine_b[me]
    weight_loads = []
    for src, dst in ((wz_in, wz), (w1_in, w1), (w2_in, w2)):
        lead = (slice(None),) * (len(src.shape) - 4)
        for j in range(src.shape[-3]):
            copy = pltpu.make_async_copy(
                src.at[lead + (slice(None), j)],
                dst.at[lead + (slice(None), slice(None), pl.ds(j * channels, channels))],
                weight_got.at[len(weight_loads)],
            )
            copy.start()
            weight_loads.append(copy)

    loads[2].wait()
    rot[...] = rotation[...].astype(F32)
    ids = source[...]
    own = onehot(ids, atoms)
    remote = onehot(ids - atoms, slots)
    order = lax.broadcasted_iota(jnp.int32, (halo, 1), 0)
    valid = jnp.concatenate(
        [(order < counts_in[:, p : p + 1]).astype(F32) for p in range(parts)], axis=0
    )
    usable = jnp.sum(remote.astype(F32) * valid, axis=0, keepdims=True)
    usable = jnp.where(ids < atoms, 1.0, usable)
    place = lax.broadcasted_iota(jnp.int32, (1, edges), 1)
    radial[...] = jnp.where(place < count[...], envelope[...] * usable, 0.0)
    to = onehot(target[...], atoms)

    g12 = {1: g1, 2: g2}
    h12 = {1: h1, 2: h2}

    def frame_grad(q, low=0, high=blocks):
        if low == 0:
            raw[...] = dot(cots[q], to, TN)

        def one(block, carry):
            e = cols(block)
            scale = radial[:, e]

            def put(degree, m, value):
                value = (value * scale).astype(BF)
                o = abs(m)
                row = pl.ds(
                    pl.multiple_of((degree - o) * channels + q * width, width), width
                )
                if o == 0:
                    gz[row, e] = value
                else:
                    g12[o][row, cols(block, 0 if m > 0 else edges)] = value

            rotate_in(rot, raw, block, width, put)
            return carry

        lax.fori_loop(low, high, one, 0)

    def one_h(low, high, block, carry):
        e = cols(block)
        later = cols(block, edges)

        def put(degree, m, value):
            value = value.astype(BF)
            o = abs(m)
            first = (degree - o) * width
            spot = 7 - o + degree - o
            if o == 2 and spot >= 8:
                spot = 11 if spot == 8 else 8
            second = spot * width
            if o == 0:
                hz[pl.ds(first, width), e] = value
            elif m > 0:
                h12[o][pl.ds(first, width), e] = value
                h12[o][pl.ds(second, width), later] = value
            else:
                h12[o][pl.ds(first, width), later] = value
                h12[o][pl.ds(second, width), e] = -value

        rotate_in(rot, raw, block, width, put, low, high)
        return carry

    spans = []
    base = 0
    for rows in (14 * share, 18 * share, 11 * share):
        spans.append(pl.ds(base, rows))
        base += rows
    near_copies = {}
    lane = lax.broadcasted_iota(jnp.int32, (1, LANES), 1)

    def weight_piece(k):
        q = steps[k]

        def left(g, count_l):
            return jnp.concatenate(
                [
                    g[pl.ds(pl.multiple_of(l * channels + q * width, width), width), :]
                    for l in range(count_l)
                ],
                axis=0,
            )

        def place(start, value):
            value = value.astype(BF)
            for degree in range(value.shape[0] // width):
                for half in range(2):
                    row = degree * width + half * share
                    at = start + degree * share
                    pieces[k, half, at : at + share, :] = value[row : row + share, :]

        left_two = left(g2, 5)
        tail = dot(left_two, h2[pl.ds(2 * LANES, LANES), :], NT)
        part = dot(left(gz, 7), hz[...], NT)
        last = jnp.concatenate([tail, pltpu.roll(tail[: 2 * width], 3 * width, 1)], axis=0)
        place(0, part[:, :LANES])
        place(7 * share, jnp.where(lane < 3 * width, part[:, LANES:], last))
        send_near(k, 0)
        part = dot(left(g1, 6), h1[...], NT)
        for tile in range(3):
            place(spans[1].start + tile * 6 * share, part[:, tile * LANES : (tile + 1) * LANES])
        send_near(k, 1)
        part = dot(left_two, h2[pl.ds(0, 2 * LANES), :], NT)
        for tile in range(2):
            place(spans[2].start + tile * 5 * share, part[:, tile * LANES : (tile + 1) * LANES])
        third = pltpu.roll(tail[3 * width : 4 * width], width, 1)
        fourth = pltpu.roll(tail[4 * width :], 2 * width, 1)
        third = jnp.where(lane < 2 * width, third, fourth)
        place(spans[2].start + 10 * share, jnp.where(lane < width, tail[2 * width : 3 * width], third))
        send_near(k, 2)

    def send_near(k, c):
        copy = push(
            pieces.at[k, 1 - side, spans[c]],
            near.at[k, spans[c]],
            near_sent.at[k, c],
            near_got.at[k, c],
            {"atoms": other},
        )
        copy.start()
        near_copies[k, c] = copy

    def relay_copy(k, c):
        return push(
            passing.at[k, spans[c]],
            relay.at[k, spans[c]],
            far_sent.at[k, c],
            relay_got.at[k, c],
            {"atoms": mate * 2 + side},
        )

    def fin_copy(k, c, slot, q):
        return push(
            passing.at[k, spans[c]],
            fin.at[slot, spans[c]],
            far_sent.at[k, c],
            fin_got.at[slot, c],
            {"atoms": q * 2 + side},
        )

    def summed(k, c):
        return pieces[k, side, spans[c]].astype(F32) + near[k, spans[c]].astype(F32)

    def pass_on(k, c):
        near_copies[k, c].wait_recv()
        if k == groups - 1:
            total[spans[c], :] = summed(k, c)
            return

        @pl.when(steps[k] == mate)
        def direct():
            passing[k, spans[c], :] = summed(k, c).astype(BF)
            fin_copy(k, c, 0, mate).start()

        @pl.when((steps[k] != mate) & jnp.logical_not(inner))
        def hand():
            passing[k, spans[c], :] = summed(k, c).astype(BF)
            relay_copy(k, c).start()

    def relay_on(k, c):
        @pl.when((steps[k] != mate) & inner)
        def join():
            relay_copy(k, c).wait_recv()
            value = summed(k, c) + relay[k, spans[c]].astype(F32)
            passing[k, spans[c], :] = value.astype(BF)
            fin_copy(k, c, 1, steps[k]).start()

    frame_grad(group)
    chan_copies[0].wait_recv()
    frame_grad(flipped(1))
    hz[...] = jnp.zeros_like(hz)
    h2[...] = jnp.zeros_like(h2)

    def whole(land):
        return land[...].astype(F32).reshape(slots, land.shape[2]).astype(BF)

    for part, (land, (low, high, span)) in enumerate(zip((land_a, land_b), halves)):
        for copy in halo_copies[part * (parts - 1) : (part + 1) * (parts - 1)]:
            copy.wait_recv()
        raw[span, :] = dot(node[span, :], own, NN) + dot(whole(land), remote, TN)
        lax.fori_loop(0, blocks, functools.partial(one_h, low, high), 0)
    weight_piece(0)

    chan_copies[1].wait_recv()
    chan_copies.append(chan_copy(2, flipped(2), 1))
    chan_copies[2].start()
    frame_grad(flipped(2))
    weight_piece(1)
    pass_on(0, 0)
    chan_copies[2].wait_recv()
    frame_grad(flipped(3), 0, blocks // 2)
    pass_on(0, 1)
    frame_grad(flipped(3), blocks // 2, blocks)
    pass_on(0, 2)
    weight_piece(2)

    for copy in weight_loads:
        copy.wait()
    fb[pl.ds(0, 7 * width), :] = dot(wz[...].reshape(7 * width, 7 * channels), gz[...], NN)
    pass_on(1, 0)
    start = 7 * width
    for count_l, w, g in ((6, w1, g1), (5, w2, g2)):
        rows = count_l * width
        real = dot(w[0].reshape(rows, count_l * channels), g[...], NN)
        imag = dot(w[1].reshape(rows, count_l * channels), g[...], NN)
        fb[pl.ds(start, rows), :] = real[:, :edges] + imag[:, edges:]
        fb[pl.ds(start + rows, rows), :] = real[:, edges:] - imag[:, :edges]
        start += 2 * rows
    pass_on(1, 1)
    for c in range(2):
        relay_on(0, c)

    def one_back(low, high, block, carry):
        rotate_out(rot, fb, block, width, y, low, high)
        return carry

    back_copies = []
    for part, (back, home, (low, high, span)) in enumerate(
        zip((back_a, back_b), (home_a, home_b), halves)
    ):
        lax.fori_loop(0, blocks, functools.partial(one_back, low, high), 0)
        terms = dot(remote, y[span, :], NT).astype(BF)
        for p in range(parts):
            back[p] = terms[p * halo : (p + 1) * halo, :]
        for k in range(1, parts):
            peer = lax.rem(me + k, parts)
            copy = push(
                back.at[peer],
                home.at[me],
                back_sent.at[part, k],
                back_got.at[part, k],
                {"atoms": peer},
            )
            copy.start()
            back_copies.append(copy)
    pass_on(1, 2)
    relay_on(0, 2)
    pass_on(2, 0)
    pass_on(2, 1)
    weight_piece(3)
    relay_on(1, 0)
    relay_on(1, 1)
    pass_on(2, 2)
    relay_on(1, 2)
    x_out[...] = dot(y[...], own, NT)
    home_a[me] = back_a[me]
    home_b[me] = back_b[me]
    relay_on(2, 0)
    relay_on(2, 1)
    relay_on(2, 2)
    pass_on(3, 0)
    pass_on(3, 1)
    pass_on(3, 2)
    for part, (home, (low, high, span)) in enumerate(zip((home_a, home_b), halves)):
        for copy in back_copies[part * (parts - 1) : (part + 1) * (parts - 1)]:
            copy.wait_recv()
        x_out[span, :] += dot(whole(home), pick, TN)

    for c in range(3):
        value = total[spans[c], :]
        for slot in range(2):
            fin_copy(0, c, slot, mate).wait_recv()
            value = value + fin[slot, spans[c]].astype(F32)
        total[spans[c], :] = value * factor

    for copy in halo_copies + chan_copies + list(near_copies.values()) + back_copies:
        copy.wait_send()
    for k in range(groups - 1):
        for c in range(3):
            relay_copy(k, c).wait_send()


def write_kernel(x, total, x_out, dz_out, d1_out, d2_out):
    x_out[...] = x[...]
    share, width = dz_out.shape[-2:]

    def cut(slot, spot):
        return total[slot * share : (slot + 1) * share, spot * width : (spot + 1) * width]

    for i in range(7):
        tile, spot = divmod(i, 4)
        for j in range(7):
            dz_out[i, j] = cut(tile * 7 + j, spot)
    for i in range(12):
        tile, spot = divmod(i, 4)
        for j in range(6):
            d1_out[i // 6, i % 6, j] = cut(14 + tile * 6 + j, spot)
    for i in range(10):
        tile, spot = divmod(i, 4)
        for j in range(5):
            if i < 8:
                where = (32 + tile * 5 + j, spot)
            elif i == 8:
                where = (7 + j, 3)
            else:
                where = (12 + j, 3) if j < 2 else (42, j - 2)
            d2_out[i // 5, i % 5, j] = cut(*where)


def call(kernel, outs, scratch=(), flops=10**8, collective=None, specs=None):
    if collective is None:
        params = pltpu.CompilerParams(vmem_limit_bytes=VMEM_LIMIT)
    else:
        params = pltpu.CompilerParams(
            vmem_limit_bytes=VMEM_LIMIT, collective_id=collective, has_side_effects=True
        )
    extra = {} if specs is None else {"in_specs": specs}
    return pl.pallas_call(
        kernel,
        out_shape=outs,
        **extra,
        scratch_shapes=list(scratch),
        compiler_params=params,
        cost_estimate=pl.CostEstimate(
            flops=flops, bytes_accessed=8 * 10**6, transcendentals=0
        ),
    )


def on_device(
    node_x,
    cotangent,
    rotation,
    envelope,
    source,
    target,
    edge_count,
    send_index,
    halo_count,
    weight_zero,
    weight_one,
    weight_two,
):
    parts = lax.axis_size("atoms")
    groups = lax.axis_size("chan")
    width = node_x.shape[1]
    channels = width * groups
    atoms = node_x.shape[2]
    halo = send_index.shape[2]
    edges = source.shape[0]
    slots = parts * halo
    rows = 49 * width
    share = channels // parts
    fast = parts == 8 and groups == 4 and share % 16 == 0 and width == 2 * share
    sds = jax.ShapeDtypeStruct

    node = node_x.reshape(rows, atoms)
    cot = cotangent.reshape(rows, atoms)
    factor = 1.0 / math.sqrt(edges * parts)
    src = source.reshape(1, edges)
    tgt = target.reshape(1, edges)
    pad = lambda n: -(-n // LANES) * LANES
    lz, l1, l2 = pad(7 * width), pad(12 * width), pad(10 * width)

    if fast:
        height = 43 * share
        vmem = pltpu.VMEM
        dma = pltpu.SemaphoreType.DMA
        grad_x, summed = call(
            functools.partial(whole_kernel, factor),
            (sds((rows, atoms), F32), sds((height, LANES), F32)),
            (
                vmem((rows, atoms), BF),
                vmem((rows, atoms), BF),
                vmem((235, edges), BF),
                vmem((parts, halo, 25 * width), BF),
                vmem((parts, halo, 24 * width), BF),
                vmem((parts, halo, 25 * width), BF),
                vmem((parts, halo, 24 * width), BF),
                vmem((groups, atoms, rows), BF),
                vmem((235, edges), F32),
                vmem((rows, edges), F32),
                vmem((1, edges), F32),
                vmem((7 * channels, edges), BF),
                vmem((6 * channels, 2 * edges), BF),
                vmem((5 * channels, 2 * edges), BF),
                vmem((lz, edges), BF),
                vmem((l1, 2 * edges), BF),
                vmem((l2, 2 * edges), BF),
                vmem((7, width, 7 * channels), BF),
                vmem((2, 6, width, 6 * channels), BF),
                vmem((2, 5, width, 5 * channels), BF),
                vmem((29 * width, edges), F32),
                vmem((rows, edges), BF),
                vmem((parts, halo, 25 * width), BF),
                vmem((parts, halo, 24 * width), BF),
                vmem((parts, halo, 25 * width), BF),
                vmem((parts, halo, 24 * width), BF),
                vmem((groups, 2, height, LANES), BF),
                vmem((groups, height, LANES), BF),
                vmem((groups, height, LANES), BF),
                vmem((groups, height, LANES), BF),
                vmem((2, height, LANES), BF),
                dma((2, parts)),
                dma((2, parts)),
                dma((3,)),
                dma((3,)),
                dma((groups, 3)),
                dma((groups, 3)),
                dma((groups, 3)),
                dma((groups, 3)),
                dma((2, 3)),
                dma((2, parts)),
                dma((2, parts)),
                dma((3,)),
                dma((18,)),
            ),
            flops=10**10,
            collective=0,
            specs=[
                pl.BlockSpec(memory_space=pltpu.HBM if far else pltpu.VMEM)
                for far in (0, 1, 1, 1, 0, 0, 0, 0, 0, 1, 1, 1)
            ],
        )(
            send_index[0],
            node,
            cot,
            rotation,
            envelope.reshape(1, edges),
            src,
            tgt,
            edge_count.reshape(1, 1),
            halo_count.reshape(1, parts),
            weight_zero.transpose(0, 2, 1, 3),
            weight_one.transpose(0, 1, 3, 2, 4),
            weight_two.transpose(0, 1, 3, 2, 4),
        )
        grad_x, dz, d1, d2 = call(
            write_kernel,
            (
                sds((rows, atoms), F32),
                sds((7, 7, share, width), F32),
                sds((2, 6, 6, share, width), F32),
                sds((2, 5, 5, share, width), F32),
            ),
        )(grad_x, summed)
        return (
            grad_x.reshape(49, width, atoms),
            dz.transpose(0, 3, 1, 2),
            d1.transpose(0, 1, 4, 2, 3),
            d2.transpose(0, 1, 4, 2, 3),
        )

    sends = send_index.reshape(slots, 1)
    send_rows, cot_rows = call(
        prep_kernel, (sds((slots, rows), BF), sds((atoms, rows), BF))
    )(sends, node, cot)
    recv = lax.all_to_all(send_rows, "atoms", split_axis=0, concat_axis=0, tiled=True)
    cots = lax.all_gather(cot_rows, "chan", axis=0, tiled=False)
    valid = (
        jnp.arange(halo, dtype=jnp.int32)[None, :] < halo_count[:, 0][:, None]
    ).astype(F32).reshape(slots, 1)
    g_shapes = (
        sds((7 * channels, edges), BF),
        sds((6 * channels, 2 * edges), BF),
        sds((5 * channels, 2 * edges), BF),
    )
    d_shapes = (
        sds((7 * channels, lz), F32),
        sds((6 * channels, l1), F32),
        sds((5 * channels, l2), F32),
    )
    made = call(
        frame_kernel,
        g_shapes + d_shapes,
        (
            pltpu.VMEM((235, edges), F32),
            pltpu.VMEM((rows, edges), F32),
            pltpu.VMEM((1, edges), F32),
            pltpu.VMEM((lz, edges), BF),
            pltpu.VMEM((l1, 2 * edges), BF),
            pltpu.VMEM((l2, 2 * edges), BF),
        ),
        flops=10**10,
    )(
        node,
        recv,
        cots,
        rotation,
        envelope.reshape(1, edges),
        src,
        tgt,
        edge_count.reshape(1, 1),
        valid,
    )
    gz, g1, g2 = made[:3]
    own, halo_rows = call(
        back_kernel,
        (sds((rows, atoms), F32), sds((slots, rows), BF)),
        (
            pltpu.VMEM((235, edges), F32),
            pltpu.VMEM((29 * width, edges), F32),
            pltpu.VMEM((rows, edges), BF),
        ),
        flops=10**10,
    )(
        gz,
        g1,
        g2,
        weight_zero.reshape(7 * width, 7 * channels),
        weight_one.reshape(12 * width, 6 * channels),
        weight_two.reshape(10 * width, 5 * channels),
        rotation,
        src,
    )
    back = lax.all_to_all(halo_rows, "atoms", split_axis=0, concat_axis=0, tiled=True)
    grad_x = call(join_kernel, sds((rows, atoms), F32))(own, back, sends)

    dz = made[3][:, : 7 * width].reshape(7, channels, 7, width)
    d1 = made[4].reshape(6, channels, 2, 6, width)
    d2 = made[5][:, : 10 * width].reshape(5, channels, 2, 5, width)
    dz = lax.psum_scatter(dz, "atoms", scatter_dimension=1, tiled=True)
    d1 = lax.psum_scatter(d1, "atoms", scatter_dimension=1, tiled=True)
    d2 = lax.psum_scatter(d2, "atoms", scatter_dimension=1, tiled=True)
    return (
        grad_x.reshape(49, width, atoms),
        dz.transpose(2, 3, 0, 1) * factor,
        d1.transpose(2, 3, 4, 0, 1) * factor,
        d2.transpose(2, 3, 4, 0, 1) * factor,
    )


def solution(mesh):
    in_specs = (
        P(None, "chan", "atoms"),
        P(None, "chan", "atoms"),
        P(None, "atoms"),
        P("atoms"),
        P("atoms"),
        P("atoms"),
        P("atoms"),
        P("atoms", None, None),
        P(None, "atoms"),
        P(None, "chan", None, None),
        P(None, None, "chan", None, None),
        P(None, None, "chan", None, None),
    )
    out_specs = (
        P(None, "chan", "atoms"),
        P(None, "chan", None, "atoms"),
        P(None, None, "chan", None, "atoms"),
        P(None, None, "chan", None, "atoms"),
    )
    return jax.shard_map(
        on_device, mesh=mesh, in_specs=in_specs, out_specs=out_specs, check_vma=False
    )
```
